32 devices in a mesh: fibre: 2 (over y), chan: 8 (over z, core), tm: 2 (over x).
Axes of the slice: x: 2, y: 2, z: 4, core: 2. Of those that a mesh axis runs over, the one named last changes fastest.
Arguments:
- raw_strain: bfloat16 [2, 2560, 512], P('tm', 'fibre', 'chan'), parts along dimension 1, may hold values from -400 to 400
- fir_taps: bfloat16 [64], replicated, may hold values from -0.75 to 0.75
- live_mask: int32 [2560], P(('fibre', 'chan')), parts along dimension 0, may hold values 0 or 1
Outputs:
- correlations: bfloat16 [2560, 256, 256], P(('fibre', 'chan'), 'tm'), parts along dimension 0
The draws below stay inside these ranges and needn't reach their ends.
There are 2 independent parts, one for each index of `fibre`. The reference program is written for one: setup_inputs(seed, part) draws one part's arguments, and reference() takes and returns one part's arrays. A program takes and returns all parts, laid end to end along the dimension named above; an argument that names none is the same for every part. Nothing has to cross between parts.
All inputs are finite; a program needn't handle non-finite values. No bound on the sum of `live_mask` on one device may be relied on, other than what follows from the above.
Results may differ from the reference program's by a relative error of at most 0.0075.
Values may be sent and summed in bfloat16 or wider, within the bound.
A program may use at most 64 MiB of HBM per device.

```python
import math
import jax
import jax.numpy as jnp
from jax import lax

OFF = 256
LAG = 128
CHB = 160
TAPS = 64
STRIDE = 4
CH = 1280
NT = 128
RAW = 512
HIST = 60
WIN = 2
N_CHAN = 8


def draw_raw_strain(key, part):
    noise_key, chan_key, envelope_key = jax.random.split(jax.random.fold_in(key, 7), 3)
    noise = jnp.clip(jax.random.normal(noise_key, (WIN, CH, RAW), jnp.float32), -4.0, 4.0)
    chan_scale = jnp.exp(jax.random.uniform(chan_key, (1, CH, 1), jnp.float32, 0.0, math.log(10.0)))
    envelope = jnp.exp(jax.random.uniform(envelope_key, (WIN, CH, RAW // TAPS, 1), jnp.float32, 0.0, math.log(10.0)))
    shaped = (noise.reshape(WIN, CH, RAW // TAPS, TAPS) * envelope).reshape(WIN, CH, RAW)
    return (shaped * chan_scale).astype(jnp.bfloat16)


def set_ends(result, key, least, high):
    shape = result.shape
    place = [jax.random.randint(jax.random.fold_in(key, axis), (), 0, shape[axis]) for axis in range(len(shape))]
    result = result.at[tuple(place)].set(least)
    longest = shape.index(max(shape))
    place[longest] = (place[longest] + 1) % shape[longest]
    return result.at[tuple(place)].set(high)


def normal_values(rng, dims, scale, bound, held_as=jnp.bfloat16):
    entries = scale * jax.random.normal(rng, dims, jnp.float32)
    return jnp.clip(entries, min=-bound, max=bound).astype(held_as)


def setup_inputs(seed: int = 0, part: int = 0) -> dict:
    arg_keys = jax.random.split(jax.random.key(seed), 4)
    part_splits = jax.random.split(jax.random.fold_in(arg_keys[3], part), 4)
    raw_strain = draw_raw_strain(jax.random.fold_in(jax.random.fold_in(arg_keys[3], part), 71), part)
    fir_taps = normal_values(arg_keys[1], (TAPS,), TAPS ** -0.5, 0.75)
    live_mask = set_ends((jax.random.randint(part_splits[2], (CH,), 0, 16) < 15).astype(jnp.int32), jax.random.fold_in(part_splits[2], 1), 0, 1)
    return dict(raw_strain=raw_strain, fir_taps=fir_taps, live_mask=live_mask)


def reference(raw_strain, fir_taps, live_mask):
    raw_values = raw_strain.astype(jnp.float32)
    padded_raw = jnp.pad(raw_values, ((0, 0), (0, 0), (HIST, 0)))
    grouped = padded_raw.reshape(WIN, CH, (HIST + RAW) // STRIDE, STRIDE)
    reversed_taps = fir_taps.astype(jnp.float32)[::-1]
    filtered = jnp.zeros((WIN, CH, NT), jnp.float32)
    for block in range(TAPS // STRIDE):
        filtered = filtered + jnp.einsum('wcns,s->wcn', grouped[:, :, block:block + NT, :], reversed_taps[block * STRIDE:(block + 1) * STRIDE], precision=lax.Precision.HIGHEST)
    decimated = filtered.astype(jnp.bfloat16).astype(jnp.float32)
    loudness = jnp.sqrt(lax.optimization_barrier(jnp.mean(decimated * decimated, axis=2)) + 1e-06)
    alive_flags = live_mask.astype(jnp.float32)
    whitened = (decimated * (alive_flags[None, :, None] / loudness[:, :, None])).astype(jnp.bfloat16).astype(jnp.float32)
    lag_count = 2 * LAG
    padded_x = jnp.pad(whitened, ((0, 0), (0, 0), (lag_count, lag_count)))
    padded_y = jnp.pad(whitened, ((0, 0), (0, OFF + 1), (LAG, LAG)))
    lag_index = jnp.arange(lag_count, dtype=jnp.int32)
    row_index = jnp.arange(NT + lag_count, dtype=jnp.int32)
    toeplitz_index = row_index[None, :] - lag_index[:, None] + lag_count
    norm_scale = 1.0 / math.sqrt(NT * WIN)

    def per_group(group_index):
        first_chan = (group_index * CHB).astype(jnp.int32)
        chosen = lax.dynamic_slice_in_dim(padded_x, first_chan, CHB, 1)
        toeplitz = chosen[:, :, toeplitz_index]
        members = first_chan + 1 + jnp.arange(CHB, dtype=jnp.int32)
        partner = jax.vmap(lambda start_row: lax.dynamic_slice_in_dim(padded_y, start_row, OFF, 1))(members)
        lag_sums = jnp.einsum('gwor,wglr->glo', partner, toeplitz, precision=lax.Precision.HIGHEST)
        return (lag_sums * norm_scale).astype(jnp.bfloat16)
    stacked = lax.map(per_group, jnp.arange(N_CHAN, dtype=jnp.int32))
    return stacked.reshape(CH, lag_count, OFF)
```

```python
import functools
import math

import jax
import jax.numpy as jnp
from jax import lax
from jax.experimental import pallas as pl
from jax.experimental.pallas import tpu as pltpu
from jax.sharding import PartitionSpec as P

OFF = 256
LAG = 128
TAPS = 64
STRIDE = 4
HIST = 60
LANES = 128
SUB = 16
VMEM_GRANT = 28 * 2**20
MESH = pl.DeviceIdType.MESH


def tap_block(taps_row, member, members, tract_len, rows):
    width = members * tract_len
    tap = lax.broadcasted_iota(jnp.int32, (TAPS, width), 0)
    lane = lax.broadcasted_iota(jnp.int32, (TAPS, width), 1)
    flip = jnp.where(tap + lane == TAPS - 1, 1.0, 0.0).astype(jnp.bfloat16)
    reversed_row = jnp.dot(
        jnp.broadcast_to(taps_row, (8, TAPS)), flip, preferred_element_type=jnp.float32
    )[0:1]
    start = (member * tract_len - HIST) % width
    rolled = pltpu.roll(
        jnp.broadcast_to(reversed_row, (rows, width)), start, 1, stride=STRIDE, stride_axis=0
    )
    row = lax.broadcasted_iota(jnp.int32, (rows, width), 0)
    local = lax.broadcasted_iota(jnp.int32, (rows, width), 1) - member * tract_len
    index = STRIDE * row + STRIDE - 1 - local
    keep = (local >= 0) & (local < tract_len) & (index >= 0) & (index < TAPS)
    return jnp.where(keep, rolled, 0.0).astype(jnp.bfloat16)


def prepare_kernel(
    n_chan,
    n_tm,
    members,
    raw_hbm,
    taps_hbm,
    mask_hbm,
    out_ref,
    raw_ref,
    taps_ref,
    mask_ref,
    packed,
    received,
    fir,
    white,
    extended,
    send_a,
    recv_a,
    send_b,
    recv_b,
    load,
):
    loads = [
        pltpu.make_async_copy(source, target, load.at[i])
        for i, (source, target) in enumerate(
            [(raw_hbm, raw_ref), (taps_hbm, taps_ref), (mask_hbm, mask_ref)]
        )
    ]
    for copy in loads:
        copy.start()
    me = lax.axis_index("chan")
    my_tm = lax.axis_index("tm")
    tract_len = raw_hbm.shape[1]
    channels, samples = white.shape
    part = channels // members
    width = members * tract_len
    outputs = tract_len // STRIDE
    reach = -(-OFF // channels)

    def signal(chan, turn):
        pl.semaphore_signal(
            barrier,
            inc=1,
            device_id={"chan": chan, "tm": lax.rem(my_tm + turn, n_tm)},
            device_id_type=MESH,
        )

    barrier = pltpu.get_barrier_semaphore()
    for step in range(1, n_chan):
        signal(lax.rem(me + step, n_chan), 0)
    for turn in range(1, n_tm):
        signal(me, turn)
        for k in range(1, reach + 1):

            @pl.when(me >= k)
            def _():
                signal(me - k, turn)

            @pl.when(me + k < n_chan)
            def _():
                signal(me + k, turn)

    fir[...] = jnp.zeros_like(fir)
    loads[1].wait()
    taps_row = taps_ref[...]
    rows = 2 * outputs
    for m in range(members):
        block = tap_block(taps_row, m, members, tract_len, rows)
        for source in range(n_chan):
            first = m * samples + source * outputs
            count = min(rows, samples - source * outputs)
            fir[first : first + count, source * width : (source + 1) * width] = block[:count]
    loads[2].wait()
    alive = mask_ref[...].astype(jnp.float32)
    diagonal = lax.broadcasted_iota(jnp.int32, (channels, channels), 0) == lax.broadcasted_iota(
        jnp.int32, (channels, channels), 1
    )
    alive_column = jnp.sum(
        jnp.where(diagonal, jnp.broadcast_to(alive, (channels, channels)), 0.0),
        axis=1,
        keepdims=True,
    )
    loads[0].wait()
    turned = raw_ref[0].astype(jnp.float32).T.astype(jnp.bfloat16)
    for block in range(n_chan):
        first = block * channels
        pieces = [turned[first + m * part : first + (m + 1) * part] for m in range(members)]
        packed[block] = jnp.concatenate(pieces, axis=1)
    near_blocks = 1
    for k in range(1, reach + 1):
        near_blocks = near_blocks + (me + n_chan - k) // n_chan + 1 - (me + k) // n_chan
    pl.semaphore_wait(barrier, n_chan - 1 + (n_tm - 1) * near_blocks)

    def spread(target, slot):
        return pltpu.make_async_remote_copy(
            src_ref=packed.at[target],
            dst_ref=received.at[me],
            send_sem=send_a.at[slot],
            recv_sem=recv_a.at[me],
            device_id={"chan": target},
            device_id_type=MESH,
        )

    ways = [(distance, side) for distance in range(n_chan - 1, 0, -1) for side in range(2)]
    for distance, side in ways:
        target = me + distance if side else me - distance

        @pl.when(target < n_chan if side else target >= 0)
        def _():
            spread(target, 2 * distance + side).start()

    received[me] = packed[me]

    for k in range(1, reach + 1):
        count = min(channels, OFF - (k - 1) * channels)

        @pl.when(me + k >= n_chan)
        def _():
            extended[k * channels : k * channels + count, :] = jnp.zeros(
                (count, extended.shape[1]), extended.dtype
            )

    for source in range(n_chan):

        @pl.when(me != source)
        def _():
            pltpu.make_async_remote_copy(
                src_ref=packed.at[source],
                dst_ref=received.at[source],
                send_sem=send_a.at[0],
                recv_sem=recv_a.at[source],
                device_id={"chan": source},
                device_id_type=MESH,
            ).wait_recv()

    tracts = jnp.concatenate([received[d] for d in range(n_chan)], axis=1)
    filtered = lax.dot_general(
        tracts, fir[...], (((1,), (1,)), ((), ())), preferred_element_type=jnp.float32
    )
    for m in range(members):
        decimated = filtered[:, m * samples : (m + 1) * samples]
        decimated = decimated.astype(jnp.bfloat16).astype(jnp.float32)
        loudness = jnp.sqrt(jnp.mean(decimated * decimated, axis=1, keepdims=True) + 1e-06)
        gain = alive_column[m * part : (m + 1) * part] / loudness
        white[m * part : (m + 1) * part, :] = (decimated * gain).astype(jnp.bfloat16)

    def share(k, turn):
        count = channels if k == 0 else min(channels, OFF - (k - 1) * channels)
        window = pl.multiple_of(my_tm * samples, LANES)
        return pltpu.make_async_remote_copy(
            src_ref=white.at[pl.ds(0, count), :],
            dst_ref=extended.at[pl.ds(k * channels, count), pl.ds(window, samples)],
            send_sem=send_b.at[k, turn],
            recv_sem=recv_b.at[k, turn],
            device_id={"chan": me - k, "tm": lax.rem(my_tm + turn, n_tm)},
            device_id_type=MESH,
        )

    pairs = [(k, t) for k in range(reach, -1, -1) for t in range(n_tm - 1, -1, -1) if k or t]
    for k, turn in pairs:

        @pl.when(me >= k)
        def _():
            share(k, turn).start()

    own = pl.multiple_of(my_tm * samples, LANES)
    extended[0:channels, pl.ds(own, samples)] = white[...]
    for distance, side in ways:
        target = me + distance if side else me - distance

        @pl.when(target < n_chan if side else target >= 0)
        def _():
            spread(target, 2 * distance + side).wait_send()

    for k, turn in pairs:

        @pl.when(me + k < n_chan)
        def _():
            share(k, turn).wait_recv()

        @pl.when(me >= k)
        def _():
            share(k, turn).wait_send()

    out_ref[...] = extended[...]


def prepare(raw_strain, fir_taps, live_mask, n_chan, n_tm):
    _, all_channels, tract_len = raw_strain.shape
    channels = all_channels // n_chan
    samples = tract_len * n_chan // STRIDE
    members = max(1, LANES // tract_len)
    part = channels // members
    width = members * tract_len
    reach = -(-OFF // channels)
    vmem = pl.BlockSpec(memory_space=pltpu.VMEM)
    hbm = pl.BlockSpec(memory_space=pltpu.HBM)
    return pl.pallas_call(
        functools.partial(prepare_kernel, n_chan, n_tm, members),
        out_shape=jax.ShapeDtypeStruct((channels + OFF, n_tm * samples), jnp.bfloat16),
        in_specs=[hbm, hbm, hbm],
        out_specs=vmem,
        scratch_shapes=[
            pltpu.VMEM((1, tract_len, all_channels), jnp.bfloat16),
            pltpu.VMEM((1, TAPS), jnp.bfloat16),
            pltpu.VMEM((1, channels), jnp.int32),
            pltpu.VMEM((n_chan, part, width), jnp.bfloat16),
            pltpu.VMEM((n_chan, part, width), jnp.bfloat16),
            pltpu.VMEM((members * samples, n_chan * width), jnp.bfloat16),
            pltpu.VMEM((channels, samples), jnp.bfloat16),
            pltpu.VMEM((channels + OFF, n_tm * samples), jnp.bfloat16),
            pltpu.SemaphoreType.DMA((2 * n_chan,)),
            pltpu.SemaphoreType.DMA((n_chan,)),
            pltpu.SemaphoreType.DMA((reach + 1, n_tm)),
            pltpu.SemaphoreType.DMA((reach + 1, n_tm)),
            pltpu.SemaphoreType.DMA((3,)),
        ],
        compiler_params=pltpu.CompilerParams(
            collective_id=0, has_side_effects=True, vmem_limit_bytes=VMEM_GRANT
        ),
        name="prepare",
    )(
        pltpu.with_memory_space_constraint(raw_strain.transpose(0, 2, 1), pltpu.HBM),
        pltpu.with_memory_space_constraint(fir_taps.reshape(1, TAPS), pltpu.HBM),
        pltpu.with_memory_space_constraint(live_mask.reshape(1, channels), pltpu.HBM),
    )


def correlate_kernel(windows, samples, lag_dev, ext_ref, out_ref, wide):
    group = pl.program_id(0)
    first_lag = lax.axis_index("tm") * lag_dev - LAG
    norm_scale = 1.0 / math.sqrt(samples * windows)
    rows = ext_ref.shape[0]

    @pl.when(group == 0)
    def _():
        wide[0:rows, :] = ext_ref[...]
        wide[rows:, :] = jnp.zeros((wide.shape[0] - rows, wide.shape[1]), wide.dtype)

    base = pl.multiple_of(group * SUB, SUB)
    own = wide[pl.ds(base, SUB), :].astype(jnp.float32)
    partners = wide[pl.ds(base, OFF), :]
    beyond = wide[pl.ds(pl.multiple_of(base + OFF, SUB), LANES), :]
    lag = first_lag + lax.broadcasted_iota(jnp.int32, (lag_dev, samples), 0)
    at = lax.broadcasted_iota(jnp.int32, (lag_dev, samples), 1) - lag
    keep = (at >= 0) & (at < samples)
    lane = lax.broadcasted_iota(jnp.int32, (lag_dev, LANES), 1)
    if lag_dev % samples == 0 and LAG % samples == 0:
        turn = None
    else:
        turn = lax.rem(first_lag + samples * (-(-LAG // samples)), samples)
    blocks = []
    for r in range(SUB):
        parts = []
        for w in range(windows):
            trace = own[r : r + 1, w * samples : (w + 1) * samples]
            if turn is not None:
                trace = pltpu.roll(jnp.broadcast_to(trace, (8, samples)), turn, 1)[0:1]
            trace = jnp.broadcast_to(trace, (lag_dev, samples))
            rolled = pltpu.roll(trace, 0, 1, stride=1, stride_axis=0)
            parts.append(jnp.where(keep, rolled, 0.0).astype(jnp.bfloat16))
        blocks.append(jnp.concatenate(parts, axis=1))
    toeplitz = jnp.concatenate(blocks, axis=0)
    contract = (((1,), (1,)), ((), ()))
    near = lax.dot_general(toeplitz, partners, contract, preferred_element_type=jnp.float32)
    far = lax.dot_general(toeplitz, beyond, contract, preferred_element_type=jnp.float32)
    for r in range(SUB):
        first = r * lag_dev
        skip = r + 1
        columns = [
            near[first : first + lag_dev, k * LANES : (k + 1) * LANES] for k in range(OFF // LANES)
        ]
        columns[0] = jnp.where(lane < skip, far[first : first + lag_dev], columns[0])
        columns = [(c * norm_scale).astype(jnp.bfloat16).astype(jnp.float32) for c in columns]
        turned = [pltpu.roll(column, LANES - skip, 1) for column in columns]
        for k in range(len(columns)):
            following = turned[(k + 1) % len(columns)]
            value = jnp.where(lane < LANES - skip, turned[k], following)
            out_ref[r, :, k * LANES : (k + 1) * LANES] = value.astype(jnp.bfloat16)


def correlate(extended, channels, windows, lag_dev):
    depth = extended.shape[1]
    samples = depth // windows
    return pl.pallas_call(
        functools.partial(correlate_kernel, windows, samples, lag_dev),
        out_shape=jax.ShapeDtypeStruct((channels, lag_dev, OFF), jnp.bfloat16),
        grid=(channels // SUB,),
        in_specs=[pl.BlockSpec(extended.shape, lambda g: (0, 0))],
        out_specs=pl.BlockSpec((SUB, lag_dev, OFF), lambda g: (g, 0, 0)),
        scratch_shapes=[pltpu.VMEM((channels - SUB + OFF + LANES, depth), jnp.bfloat16)],
        compiler_params=pltpu.CompilerParams(vmem_limit_bytes=VMEM_GRANT),
        name="correlate",
    )(extended)


def shards(raw_strain, fir_taps, live_mask):
    n_chan = lax.axis_size("chan")
    n_tm = lax.axis_size("tm")
    extended = prepare(raw_strain, fir_taps, live_mask, n_chan, n_tm)
    return correlate(extended, live_mask.shape[0], n_tm, 2 * LAG // n_tm)


def solution(mesh):
    placed = (P("tm", "fibre", "chan"), P(), P(("fibre", "chan")))
    return jax.shard_map(
        shards,
        mesh=mesh,
        in_specs=placed,
        out_specs=P(("fibre", "chan"), "tm", None),
        check_vma=False,
    )
```

```python
import functools
import math

import jax
import jax.numpy as jnp
from jax import lax
from jax.experimental import pallas as pl
from jax.experimental.pallas import tpu as pltpu
from jax.sharding import PartitionSpec as P

OFF = 256
LAG = 128
TAPS = 64
STRIDE = 4
HIST = 60
LANES = 128
SUB = 16
STAGED_CHANNELS = 256
VMEM_GRANT = 28 * 2**20
MESH = pl.DeviceIdType.MESH


def tap_block(taps_row, member, members, tract_len, rows):
    width = members * tract_len
    tap = lax.broadcasted_iota(jnp.int32, (TAPS, width), 0)
    lane = lax.broadcasted_iota(jnp.int32, (TAPS, width), 1)
    flip = jnp.where(tap + lane == TAPS - 1, 1.0, 0.0).astype(jnp.bfloat16)
    reversed_row = jnp.dot(
        jnp.broadcast_to(taps_row, (8, TAPS)), flip, preferred_element_type=jnp.float32
    )[0:1]
    start = (member * tract_len - HIST) % width
    rolled = pltpu.roll(
        jnp.broadcast_to(reversed_row, (rows, width)), start, 1, stride=STRIDE, stride_axis=0
    )
    row = lax.broadcasted_iota(jnp.int32, (rows, width), 0)
    local = lax.broadcasted_iota(jnp.int32, (rows, width), 1) - member * tract_len
    index = STRIDE * row + STRIDE - 1 - local
    keep = (local >= 0) & (local < tract_len) & (index >= 0) & (index < TAPS)
    return jnp.where(keep, rolled, 0.0).astype(jnp.bfloat16)


def prepare_kernel(
    n_chan,
    n_tm,
    members,
    raw_hbm,
    taps_hbm,
    mask_hbm,
    out_ref,
    raw_ref,
    taps_ref,
    mask_ref,
    packed,
    received,
    fir,
    white,
    extended,
    send_a,
    recv_a,
    send_b,
    recv_b,
    load,
):
    loads = [
        pltpu.make_async_copy(source, target, load.at[i])
        for i, (source, target) in enumerate(
            [(raw_hbm, raw_ref), (taps_hbm, taps_ref), (mask_hbm, mask_ref)]
        )
    ]
    for copy in loads:
        copy.start()
    me = lax.axis_index("chan")
    my_tm = lax.axis_index("tm")
    tract_len = raw_hbm.shape[1]
    channels, samples = white.shape
    part = channels // members
    width = members * tract_len
    outputs = tract_len // STRIDE
    reach = -(-OFF // channels)

    def signal(chan, turn):
        pl.semaphore_signal(
            barrier,
            inc=1,
            device_id={"chan": chan, "tm": lax.rem(my_tm + turn, n_tm)},
            device_id_type=MESH,
        )

    barrier = pltpu.get_barrier_semaphore()
    for step in range(1, n_chan):
        signal(lax.rem(me + step, n_chan), 0)
    for turn in range(1, n_tm):
        signal(me, turn)
        for k in range(1, reach + 1):

            @pl.when(me >= k)
            def _():
                signal(me - k, turn)

            @pl.when(me + k < n_chan)
            def _():
                signal(me + k, turn)

    fir[...] = jnp.zeros_like(fir)
    loads[1].wait()
    taps_row = taps_ref[...]
    rows = 2 * outputs
    for m in range(members):
        block = tap_block(taps_row, m, members, tract_len, rows)
        for source in range(n_chan):
            first = m * samples + source * outputs
            count = min(rows, samples - source * outputs)
            fir[first : first + count, source * width : (source + 1) * width] = block[:count]
    loads[2].wait()
    alive = mask_ref[...].astype(jnp.float32)
    diagonal = lax.broadcasted_iota(jnp.int32, (channels, channels), 0) == lax.broadcasted_iota(
        jnp.int32, (channels, channels), 1
    )
    alive_column = jnp.sum(
        jnp.where(diagonal, jnp.broadcast_to(alive, (channels, channels)), 0.0),
        axis=1,
        keepdims=True,
    )
    loads[0].wait()
    turned = raw_ref[0].astype(jnp.float32).T.astype(jnp.bfloat16)
    for block in range(n_chan):
        first = block * channels
        pieces = [turned[first + m * part : first + (m + 1) * part] for m in range(members)]
        packed[block] = jnp.concatenate(pieces, axis=1)
    near_blocks = 1
    for k in range(1, reach + 1):
        near_blocks = near_blocks + (me + n_chan - k) // n_chan + 1 - (me + k) // n_chan
    pl.semaphore_wait(barrier, n_chan - 1 + (n_tm - 1) * near_blocks)

    def spread(target, slot):
        return pltpu.make_async_remote_copy(
            src_ref=packed.at[target],
            dst_ref=received.at[me],
            send_sem=send_a.at[slot],
            recv_sem=recv_a.at[me],
            device_id={"chan": target},
            device_id_type=MESH,
        )

    ways = [(distance, side) for distance in range(n_chan - 1, 0, -1) for side in range(2)]
    for distance, side in ways:
        target = me + distance if side else me - distance

        @pl.when(target < n_chan if side else target >= 0)
        def _():
            spread(target, 2 * distance + side).start()

    received[me] = packed[me]

    for k in range(1, reach + 1):
        count = min(channels, OFF - (k - 1) * channels)

        @pl.when(me + k >= n_chan)
        def _():
            extended[k * channels : k * channels + count, :] = jnp.zeros(
                (count, extended.shape[1]), extended.dtype
            )

    for source in range(n_chan):

        @pl.when(me != source)
        def _():
            pltpu.make_async_remote_copy(
                src_ref=packed.at[source],
                dst_ref=received.at[source],
                send_sem=send_a.at[0],
                recv_sem=recv_a.at[source],
                device_id={"chan": source},
                device_id_type=MESH,
            ).wait_recv()

    tracts = jnp.concatenate([received[d] for d in range(n_chan)], axis=1)
    filtered = lax.dot_general(
        tracts, fir[...], (((1,), (1,)), ((), ())), preferred_element_type=jnp.float32
    )
    for m in range(members):
        decimated = filtered[:, m * samples : (m + 1) * samples]
        decimated = decimated.astype(jnp.bfloat16).astype(jnp.float32)
        loudness = jnp.sqrt(jnp.mean(decimated * decimated, axis=1, keepdims=True) + 1e-06)
        gain = alive_column[m * part : (m + 1) * part] / loudness
        white[m * part : (m + 1) * part, :] = (decimated * gain).astype(jnp.bfloat16)

    def share(k, turn):
        count = channels if k == 0 else min(channels, OFF - (k - 1) * channels)
        window = pl.multiple_of(my_tm * samples, LANES)
        return pltpu.make_async_remote_copy(
            src_ref=white.at[pl.ds(0, count), :],
            dst_ref=extended.at[pl.ds(k * channels, count), pl.ds(window, samples)],
            send_sem=send_b.at[k, turn],
            recv_sem=recv_b.at[k, turn],
            device_id={"chan": me - k, "tm": lax.rem(my_tm + turn, n_tm)},
            device_id_type=MESH,
        )

    pairs = [(k, t) for k in range(reach, -1, -1) for t in range(n_tm - 1, -1, -1) if k or t]
    for k, turn in pairs:

        @pl.when(me >= k)
        def _():
            share(k, turn).start()

    own = pl.multiple_of(my_tm * samples, LANES)
    extended[0:channels, pl.ds(own, samples)] = white[...]
    for distance, side in ways:
        target = me + distance if side else me - distance

        @pl.when(target < n_chan if side else target >= 0)
        def _():
            spread(target, 2 * distance + side).wait_send()

    for k, turn in pairs:

        @pl.when(me + k < n_chan)
        def _():
            share(k, turn).wait_recv()

        @pl.when(me >= k)
        def _():
            share(k, turn).wait_send()

    out_ref[...] = extended[...]


def prepare(raw_strain, fir_taps, live_mask, n_chan, n_tm):
    _, all_channels, tract_len = raw_strain.shape
    channels = all_channels // n_chan
    samples = tract_len * n_chan // STRIDE
    members = max(1, LANES // tract_len)
    part = channels // members
    width = members * tract_len
    reach = -(-OFF // channels)
    vmem = pl.BlockSpec(memory_space=pltpu.VMEM)
    hbm = pl.BlockSpec(memory_space=pltpu.HBM)
    return pl.pallas_call(
        functools.partial(prepare_kernel, n_chan, n_tm, members),
        out_shape=jax.ShapeDtypeStruct((channels + OFF, n_tm * samples), jnp.bfloat16),
        in_specs=[hbm, hbm, hbm],
        out_specs=vmem,
        scratch_shapes=[
            pltpu.VMEM((1, tract_len, all_channels), jnp.bfloat16),
            pltpu.VMEM((1, TAPS), jnp.bfloat16),
            pltpu.VMEM((1, channels), jnp.int32),
            pltpu.VMEM((n_chan, part, width), jnp.bfloat16),
            pltpu.VMEM((n_chan, part, width), jnp.bfloat16),
            pltpu.VMEM((members * samples, n_chan * width), jnp.bfloat16),
            pltpu.VMEM((channels, samples), jnp.bfloat16),
            pltpu.VMEM((channels + OFF, n_tm * samples), jnp.bfloat16),
            pltpu.SemaphoreType.DMA((2 * n_chan,)),
            pltpu.SemaphoreType.DMA((n_chan,)),
            pltpu.SemaphoreType.DMA((reach + 1, n_tm)),
            pltpu.SemaphoreType.DMA((reach + 1, n_tm)),
            pltpu.SemaphoreType.DMA((3,)),
        ],
        compiler_params=pltpu.CompilerParams(
            collective_id=0, has_side_effects=True, vmem_limit_bytes=VMEM_GRANT
        ),
        name="prepare",
    )(
        pltpu.with_memory_space_constraint(raw_strain.transpose(0, 2, 1), pltpu.HBM),
        pltpu.with_memory_space_constraint(fir_taps.reshape(1, TAPS), pltpu.HBM),
        pltpu.with_memory_space_constraint(live_mask.reshape(1, channels), pltpu.HBM),
    )


def correlate_kernel(windows, samples, lag_dev, ext_ref, out_ref, wide):
    group = pl.program_id(0)
    first_lag = lax.axis_index("tm") * lag_dev - LAG
    norm_scale = 1.0 / math.sqrt(samples * windows)
    rows = ext_ref.shape[0]

    @pl.when(group == 0)
    def _():
        wide[0:rows, :] = ext_ref[...]
        wide[rows:, :] = jnp.zeros((wide.shape[0] - rows, wide.shape[1]), wide.dtype)

    base = pl.multiple_of(group * SUB, SUB)
    own = wide[pl.ds(base, SUB), :].astype(jnp.float32)
    partners = wide[pl.ds(base, OFF), :]
    beyond = wide[pl.ds(pl.multiple_of(base + OFF, SUB), LANES), :]
    lag = first_lag + lax.broadcasted_iota(jnp.int32, (lag_dev, samples), 0)
    at = lax.broadcasted_iota(jnp.int32, (lag_dev, samples), 1) - lag
    keep = (at >= 0) & (at < samples)
    lane = lax.broadcasted_iota(jnp.int32, (lag_dev, LANES), 1)
    if lag_dev % samples == 0 and LAG % samples == 0:
        turn = None
    else:
        turn = lax.rem(first_lag + samples * (-(-LAG // samples)), samples)
    blocks = []
    for r in range(SUB):
        parts = []
        for w in range(windows):
            trace = own[r : r + 1, w * samples : (w + 1) * samples]
            if turn is not None:
                trace = pltpu.roll(jnp.broadcast_to(trace, (8, samples)), turn, 1)[0:1]
            trace = jnp.broadcast_to(trace, (lag_dev, samples))
            rolled = pltpu.roll(trace, 0, 1, stride=1, stride_axis=0)
            parts.append(jnp.where(keep, rolled, 0.0).astype(jnp.bfloat16))
        blocks.append(jnp.concatenate(parts, axis=1))
    toeplitz = jnp.concatenate(blocks, axis=0)
    contract = (((1,), (1,)), ((), ()))
    near = lax.dot_general(toeplitz, partners, contract, preferred_element_type=jnp.float32)
    far = lax.dot_general(toeplitz, beyond, contract, preferred_element_type=jnp.float32)
    for r in range(SUB):
        first = r * lag_dev
        skip = r + 1
        columns = [
            near[first : first + lag_dev, k * LANES : (k + 1) * LANES] for k in range(OFF // LANES)
        ]
        columns[0] = jnp.where(lane < skip, far[first : first + lag_dev], columns[0])
        columns = [(c * norm_scale).astype(jnp.bfloat16).astype(jnp.float32) for c in columns]
        turned = [pltpu.roll(column, LANES - skip, 1) for column in columns]
        for k in range(len(columns)):
            following = turned[(k + 1) % len(columns)]
            value = jnp.where(lane < LANES - skip, turned[k], following)
            out_ref[r, :, k * LANES : (k + 1) * LANES] = value.astype(jnp.bfloat16)


def correlate(extended, channels, windows, lag_dev):
    depth = extended.shape[1]
    samples = depth // windows
    return pl.pallas_call(
        functools.partial(correlate_kernel, windows, samples, lag_dev),
        out_shape=jax.ShapeDtypeStruct((channels, lag_dev, OFF), jnp.bfloat16),
        grid=(channels // SUB,),
        in_specs=[pl.BlockSpec(extended.shape, lambda g: (0, 0))],
        out_specs=pl.BlockSpec((SUB, lag_dev, OFF), lambda g: (g, 0, 0)),
        scratch_shapes=[pltpu.VMEM((channels - SUB + OFF + LANES, depth), jnp.bfloat16)],
        compiler_params=pltpu.CompilerParams(vmem_limit_bytes=VMEM_GRANT),
        name="correlate",
    )(extended)


def sweep_kernel(windows, samples, ext_ref, out_ref, traces, plane, staged, ship_sem):
    positive = lax.axis_index("tm")
    channels, lag_dev, _ = staged.shape
    depth = windows * samples
    pad = samples - SUB
    width = plane.shape[2]
    scale = 1.0 / math.sqrt(depth)
    missing = jnp.zeros((width - ext_ref.shape[0], depth), jnp.float32)
    turned = jnp.concatenate([ext_ref[...].astype(jnp.float32), missing], axis=0)
    turned = turned.T.astype(jnp.bfloat16)
    for w in range(windows):
        plane[w, 0:pad, :] = jnp.zeros((pad, width), jnp.bfloat16)
        plane[w, pad + samples :, :] = jnp.zeros((pad, width), jnp.bfloat16)
        plane[w, pad : pad + samples, :] = turned[w * samples : (w + 1) * samples]
    row = lax.broadcasted_iota(jnp.int32, (SUB, samples), 0)
    at = lax.broadcasted_iota(jnp.int32, (SUB, samples), 1) - row + SUB * (1 - positive)
    weight = jnp.where((at >= 0) & (at < samples), scale, 0.0)
    shift = (1 - positive) * pad
    for first in range(0, channels, SUB):
        own = ext_ref[first : first + SUB, :].astype(jnp.float32)
        for w in range(windows):
            lanes = slice(w * samples, (w + 1) * samples)
            moved = pltpu.roll(own[:, lanes], shift, 1)
            for r in range(SUB):
                trace = jnp.broadcast_to(moved[r : r + 1], (SUB, samples))
                rolled = pltpu.roll(trace, 0, 1, stride=1, stride_axis=0)
                traces[first + r, :, lanes] = (rolled * weight).astype(jnp.bfloat16)

    lane = lax.broadcasted_iota(jnp.int32, (SUB, LANES), 1)
    half = SUB // 2
    groups = channels // (2 * SUB)
    steps = lag_dev // (2 * SUB) * groups

    def place(turn):
        step, odd = divmod(turn, 2)
        return (2 * (step % groups) + odd) * SUB, 2 * (step // groups)

    def weights(turn, band, first_lane, count):
        channel, low = place(turn)
        start = pl.multiple_of((low + band) * SUB + positive * pad, SUB)
        lanes = channel // LANES * LANES + first_lane
        return jnp.concatenate(
            [plane[w, pl.ds(start, samples), lanes : lanes + count] for w in range(windows)], axis=0
        )

    def finish(turn, accs, i):
        channel, low = place(turn)
        part, k = divmod(i, half)
        near = [pltpu.matmul_pop(accs[turn % 2][unit][part][k]) for unit in range(2)]
        far = pltpu.matmul_pop(accs[turn % 2][part][2][k])
        skip = (channel + i) % LANES + 1
        for band in range(2):
            columns = [
                near[band][:, :LANES],
                near[band][:, LANES:],
                far[:, band * LANES : (band + 1) * LANES],
            ]
            values = [
                pltpu.roll(jnp.where(lane < skip, columns[k + 1], columns[k]), LANES - skip, 1)
                for k in range(2)
            ]
            first = (low + band) * SUB
            staged[channel + i, first : first + SUB, :] = jnp.concatenate(values, axis=1).astype(
                jnp.bfloat16
            )

    def launch(turn, accs):
        channel, _ = place(turn)
        odd = turn % 2
        if not odd:
            for unit in range(2):
                pltpu.matmul_push_rhs(weights(turn, unit, 0, OFF), 0, unit)
        count = done = 0
        for kind in (2, 0, 1) if odd else (0, 1, 2):
            for i in range(half):
                staged_rhs = None
                if i == 0 and kind == 0:
                    staged_rhs = 0
                elif i == 0 and kind == 2 and not odd:
                    staged_rhs = 1
                for unit in range(2):
                    part = unit if kind == 2 else kind
                    pltpu.matmul_acc_lhs(
                        accs[odd][unit][kind][i],
                        traces[channel + part * half + i],
                        load_staged_rhs=staged_rhs,
                    )
                if i == 0 and kind == 0 and not odd:
                    for unit in range(2):
                        far = [weights(turn, band, OFF, LANES) for band in range(2)]
                        pltpu.matmul_push_rhs(jnp.concatenate(far, axis=1), 1, unit)
                if i == 0 and kind == 2 and odd:
                    for unit in range(2):
                        pltpu.matmul_push_rhs(weights(turn, unit, 0, OFF), 0, unit)
                count += 1
                while turn and done < SUB * count // (3 * half):
                    finish(turn - 1, accs, done)
                    done += 1

    def ship(step):
        channel, low = place(2 * step)
        where = (pl.ds(channel, 2 * SUB), pl.ds(low * SUB, 2 * SUB), slice(None))
        return pltpu.make_async_copy(staged.at[where], out_ref.at[where], ship_sem.at[step])

    def run(*flat):
        flat = iter(flat)
        accs = [[[None] * 3 for _ in range(2)] for _ in range(2)]
        for odd in range(2):
            for unit in range(2):
                for kind in range(3):
                    accs[odd][unit][kind] = [next(flat) for _ in range(half)]
        for turn in range(2 * steps):
            launch(turn, accs)
            if turn and turn % 2 == 0:
                ship(turn // 2 - 1).start()
        for i in range(SUB):
            finish(2 * steps - 1, accs, i)
        ship(steps - 1).start()

    pl.run_scoped(
        run,
        *[
            pltpu.ACC(unit)((SUB, OFF), jnp.float32)
            for odd in range(2)
            for unit in range(2)
            for _ in range(3 * half)
        ],
    )
    for step in range(steps):
        ship(step).wait()


def sweep(extended, channels, windows, lag_dev):
    rows, depth = extended.shape
    samples = depth // windows
    width = -(-rows // LANES) * LANES
    steps = lag_dev // (2 * SUB) * (channels // (2 * SUB))
    return pl.pallas_call(
        functools.partial(sweep_kernel, windows, samples),
        out_shape=jax.ShapeDtypeStruct((channels, lag_dev, OFF), jnp.bfloat16),
        in_specs=[pl.BlockSpec(memory_space=pltpu.VMEM)],
        out_specs=pl.BlockSpec(memory_space=pltpu.HBM),
        scratch_shapes=[
            pltpu.VMEM((channels, SUB, depth), jnp.bfloat16),
            pltpu.VMEM((windows, 3 * samples - 2 * SUB, width), jnp.bfloat16),
            pltpu.VMEM((channels, lag_dev, OFF), jnp.bfloat16),
            pltpu.SemaphoreType.DMA((steps,)),
        ],
        compiler_params=pltpu.CompilerParams(vmem_limit_bytes=VMEM_GRANT),
        name="sweep",
    )(extended)


def shards(raw_strain, fir_taps, live_mask):
    n_chan = lax.axis_size("chan")
    n_tm = lax.axis_size("tm")
    channels = live_mask.shape[0]
    lag_dev = 2 * LAG // n_tm
    extended = prepare(raw_strain, fir_taps, live_mask, n_chan, n_tm)
    whole_window = n_tm == 2 and extended.shape[1] == n_tm * LAG == OFF
    if whole_window and channels % (2 * SUB) == 0 and channels <= STAGED_CHANNELS:
        return sweep(extended, channels, n_tm, lag_dev)
    return correlate(extended, channels, n_tm, lag_dev)


def solution(mesh):
    placed = (P("tm", "fibre", "chan"), P(), P(("fibre", "chan")))
    return jax.shard_map(
        shards,
        mesh=mesh,
        in_specs=placed,
        out_specs=P(("fibre", "chan"), "tm", None),
        check_vma=False,
    )
```

```python
import functools
import math

import jax
import jax.numpy as jnp
from jax import lax
from jax.experimental import pallas as pl
from jax.experimental.pallas import tpu as pltpu
from jax.sharding import PartitionSpec as P

OFF = 256
LAG = 128
TAPS = 64
STRIDE = 4
HIST = 60
LANES = 128
SUB = 16
STAGED_CHANNELS = 256
VMEM_GRANT = 28 * 2**20
MESH = pl.DeviceIdType.MESH


def tap_block(taps_row, member, members, tract_len, rows):
    width = members * tract_len
    tap = lax.broadcasted_iota(jnp.int32, (TAPS, width), 0)
    lane = lax.broadcasted_iota(jnp.int32, (TAPS, width), 1)
    flip = jnp.where(tap + lane == TAPS - 1, 1.0, 0.0).astype(jnp.bfloat16)
    reversed_row = jnp.dot(
        jnp.broadcast_to(taps_row, (8, TAPS)), flip, preferred_element_type=jnp.float32
    )[0:1]
    start = (member * tract_len - HIST) % width
    rolled = pltpu.roll(
        jnp.broadcast_to(reversed_row, (rows, width)), start, 1, stride=STRIDE, stride_axis=0
    )
    row = lax.broadcasted_iota(jnp.int32, (rows, width), 0)
    local = lax.broadcasted_iota(jnp.int32, (rows, width), 1) - member * tract_len
    index = STRIDE * row + STRIDE - 1 - local
    keep = (local >= 0) & (local < tract_len) & (index >= 0) & (index < TAPS)
    return jnp.where(keep, rolled, 0.0).astype(jnp.bfloat16)


def prepare_kernel(
    n_chan,
    n_tm,
    members,
    outs,
    raw_hbm,
    taps_hbm,
    mask_hbm,
    *refs,
):
    out_refs, refs = refs[:outs], refs[outs:]
    (
        raw_ref,
        taps_ref,
        mask_ref,
        packed,
        received,
        fir,
        white,
        extended,
        send_a,
        recv_a,
        send_b,
        recv_b,
        load,
    ) = refs
    loads = [
        pltpu.make_async_copy(source, target, load.at[i])
        for i, (source, target) in enumerate(
            [(raw_hbm, raw_ref), (taps_hbm, taps_ref), (mask_hbm, mask_ref)]
        )
    ]
    for copy in loads:
        copy.start()
    me = lax.axis_index("chan")
    my_tm = lax.axis_index("tm")
    tract_len = raw_hbm.shape[1]
    channels, samples = white.shape
    part = channels // members
    width = members * tract_len
    outputs = tract_len // STRIDE
    reach = -(-OFF // channels)

    def signal(chan, turn):
        pl.semaphore_signal(
            barrier,
            inc=1,
            device_id={"chan": chan, "tm": lax.rem(my_tm + turn, n_tm)},
            device_id_type=MESH,
        )

    barrier = pltpu.get_barrier_semaphore()
    for step in range(1, n_chan):
        signal(lax.rem(me + step, n_chan), 0)
    for turn in range(1, n_tm):
        signal(me, turn)
        for k in range(1, reach + 1):

            @pl.when(me >= k)
            def _():
                signal(me - k, turn)

            @pl.when(me + k < n_chan)
            def _():
                signal(me + k, turn)

    fir[...] = jnp.zeros_like(fir)
    loads[1].wait()
    taps_row = taps_ref[...]
    rows = 2 * outputs
    for m in range(members):
        block = tap_block(taps_row, m, members, tract_len, rows)
        for source in range(n_chan):
            first = m * samples + source * outputs
            count = min(rows, samples - source * outputs)
            fir[first : first + count, source * width : (source + 1) * width] = block[:count]
    loads[2].wait()
    alive = mask_ref[...].astype(jnp.float32)
    diagonal = lax.broadcasted_iota(jnp.int32, (channels, channels), 0) == lax.broadcasted_iota(
        jnp.int32, (channels, channels), 1
    )
    alive_column = jnp.sum(
        jnp.where(diagonal, jnp.broadcast_to(alive, (channels, channels)), 0.0),
        axis=1,
        keepdims=True,
    )
    loads[0].wait()
    turned = raw_ref[0].astype(jnp.float32).T.astype(jnp.bfloat16)
    for block in range(n_chan):
        first = block * channels
        pieces = [turned[first + m * part : first + (m + 1) * part] for m in range(members)]
        packed[block] = jnp.concatenate(pieces, axis=1)
    near_blocks = 1
    for k in range(1, reach + 1):
        near_blocks = near_blocks + (me + n_chan - k) // n_chan + 1 - (me + k) // n_chan
    pl.semaphore_wait(barrier, n_chan - 1 + (n_tm - 1) * near_blocks)

    def spread(target, slot):
        return pltpu.make_async_remote_copy(
            src_ref=packed.at[target],
            dst_ref=received.at[me],
            send_sem=send_a.at[slot],
            recv_sem=recv_a.at[me],
            device_id={"chan": target},
            device_id_type=MESH,
        )

    ways = [(distance, side) for distance in range(n_chan - 1, 0, -1) for side in range(2)]
    for distance, side in ways:
        target = me + distance if side else me - distance

        @pl.when(target < n_chan if side else target >= 0)
        def _():
            spread(target, 2 * distance + side).start()

    received[me] = packed[me]

    for k in range(1, reach + 1):
        count = min(channels, OFF - (k - 1) * channels)

        @pl.when(me + k >= n_chan)
        def _():
            extended[k * channels : k * channels + count, :] = jnp.zeros(
                (count, extended.shape[1]), extended.dtype
            )

    if len(out_refs) > 1:
        traces, plane = out_refs
        pad = samples - SUB
        for w in range(n_tm):
            plane[w, 0:pad, :] = jnp.zeros((pad, plane.shape[2]), plane.dtype)
            plane[w, pad + samples :, :] = jnp.zeros((pad, plane.shape[2]), plane.dtype)
        tail = extended.shape[0] - channels - OFF
        if tail:
            extended[channels + OFF :, :] = jnp.zeros((tail, extended.shape[1]), extended.dtype)

    for source in range(n_chan):

        @pl.when(me != source)
        def _():
            pltpu.make_async_remote_copy(
                src_ref=packed.at[source],
                dst_ref=received.at[source],
                send_sem=send_a.at[0],
                recv_sem=recv_a.at[source],
                device_id={"chan": source},
                device_id_type=MESH,
            ).wait_recv()

    tracts = jnp.concatenate([received[d] for d in range(n_chan)], axis=1)
    filtered = lax.dot_general(
        tracts, fir[...], (((1,), (1,)), ((), ())), preferred_element_type=jnp.float32
    )
    for m in range(members):
        decimated = filtered[:, m * samples : (m + 1) * samples]
        decimated = decimated.astype(jnp.bfloat16).astype(jnp.float32)
        loudness = jnp.sqrt(jnp.mean(decimated * decimated, axis=1, keepdims=True) + 1e-06)
        gain = alive_column[m * part : (m + 1) * part] / loudness
        white[m * part : (m + 1) * part, :] = (decimated * gain).astype(jnp.bfloat16)

    def share(k, turn):
        count = channels if k == 0 else min(channels, OFF - (k - 1) * channels)
        window = pl.multiple_of(my_tm * samples, LANES)
        return pltpu.make_async_remote_copy(
            src_ref=white.at[pl.ds(0, count), :],
            dst_ref=extended.at[pl.ds(k * channels, count), pl.ds(window, samples)],
            send_sem=send_b.at[k, turn],
            recv_sem=recv_b.at[k, turn],
            device_id={"chan": me - k, "tm": lax.rem(my_tm + turn, n_tm)},
            device_id_type=MESH,
        )

    pairs = [(k, t) for k in range(reach, -1, -1) for t in range(n_tm - 1, -1, -1) if k or t]
    for k, turn in pairs:

        @pl.when(me >= k)
        def _():
            share(k, turn).start()

    own = pl.multiple_of(my_tm * samples, LANES)
    extended[0:channels, pl.ds(own, samples)] = white[...]
    if len(out_refs) > 1:
        traces, plane = out_refs
        lay_rows(white[...], traces, own, my_tm, n_tm)
    tiles = extended.shape[0] // LANES
    laid = 0
    for k in range(reach + 1):
        for turn in range(n_tm):
            if k == 0 and turn == 0:
                continue

            @pl.when(me + k < n_chan)
            def _():
                share(k, turn).wait_recv()

        if len(out_refs) == 1:
            continue
        if k == 0:
            for turn in range(1, n_tm):
                window = lax.rem(my_tm + n_tm - turn, n_tm)
                lanes = pl.multiple_of(window * samples, LANES)
                lay_rows(extended[0:channels, pl.ds(lanes, samples)], traces, lanes, my_tm, n_tm)
        ready = tiles if k == reach else (k + 1) * channels // LANES
        for tile in range(laid, ready):
            lanes = slice(tile * LANES, (tile + 1) * LANES)
            turned = extended[lanes, :].astype(jnp.float32).T.astype(jnp.bfloat16)
            for w in range(n_tm):
                plane[w, samples - SUB : 2 * samples - SUB, lanes] = turned[
                    w * samples : (w + 1) * samples
                ]
        laid = ready

    for distance, side in ways:
        target = me + distance if side else me - distance

        @pl.when(target < n_chan if side else target >= 0)
        def _():
            spread(target, 2 * distance + side).wait_send()

    for k, turn in pairs:

        @pl.when(me >= k)
        def _():
            share(k, turn).wait_send()

    if len(out_refs) == 1:
        out_refs[0][...] = extended[...]


def lay_rows(own, traces, lanes, my_tm, n_tm):
    channels, samples = own.shape
    positive = my_tm
    scale = 1.0 / math.sqrt(samples * n_tm)
    row = lax.broadcasted_iota(jnp.int32, (SUB, samples), 0)
    at = lax.broadcasted_iota(jnp.int32, (SUB, samples), 1) - row + SUB * (1 - positive)
    weight = jnp.where((at >= 0) & (at < samples), scale, 0.0)
    moved = pltpu.roll(own.astype(jnp.float32), (1 - positive) * (samples - SUB), 1)
    for channel in range(channels):
        trace = jnp.broadcast_to(moved[channel : channel + 1], (SUB, samples))
        rolled = pltpu.roll(trace, 0, 1, stride=1, stride_axis=0)
        traces[channel, :, pl.ds(lanes, samples)] = (rolled * weight).astype(jnp.bfloat16)


def prepare(raw_strain, fir_taps, live_mask, n_chan, n_tm, swept):
    _, all_channels, tract_len = raw_strain.shape
    channels = all_channels // n_chan
    samples = tract_len * n_chan // STRIDE
    members = max(1, LANES // tract_len)
    part = channels // members
    width = members * tract_len
    reach = -(-OFF // channels)
    vmem = pl.BlockSpec(memory_space=pltpu.VMEM)
    hbm = pl.BlockSpec(memory_space=pltpu.HBM)
    landing = channels + OFF
    outs = [(landing, n_tm * samples)]
    if swept:
        landing = -(-landing // LANES) * LANES
        outs = [
            (channels, SUB, n_tm * samples),
            (n_tm, 3 * samples - 2 * SUB, landing),
        ]
    return pl.pallas_call(
        functools.partial(prepare_kernel, n_chan, n_tm, members, len(outs)),
        out_shape=[jax.ShapeDtypeStruct(shape, jnp.bfloat16) for shape in outs],
        in_specs=[hbm, hbm, hbm],
        out_specs=[vmem] * len(outs),
        scratch_shapes=[
            pltpu.VMEM((1, tract_len, all_channels), jnp.bfloat16),
            pltpu.VMEM((1, TAPS), jnp.bfloat16),
            pltpu.VMEM((1, channels), jnp.int32),
            pltpu.VMEM((n_chan, part, width), jnp.bfloat16),
            pltpu.VMEM((n_chan, part, width), jnp.bfloat16),
            pltpu.VMEM((members * samples, n_chan * width), jnp.bfloat16),
            pltpu.VMEM((channels, samples), jnp.bfloat16),
            pltpu.VMEM((landing, n_tm * samples), jnp.bfloat16),
            pltpu.SemaphoreType.DMA((2 * n_chan,)),
            pltpu.SemaphoreType.DMA((n_chan,)),
            pltpu.SemaphoreType.DMA((reach + 1, n_tm)),
            pltpu.SemaphoreType.DMA((reach + 1, n_tm)),
            pltpu.SemaphoreType.DMA((3,)),
        ],
        compiler_params=pltpu.CompilerParams(
            collective_id=0, has_side_effects=True, vmem_limit_bytes=VMEM_GRANT
        ),
        name="prepare",
    )(
        pltpu.with_memory_space_constraint(raw_strain.transpose(0, 2, 1), pltpu.HBM),
        pltpu.with_memory_space_constraint(fir_taps.reshape(1, TAPS), pltpu.HBM),
        pltpu.with_memory_space_constraint(live_mask.reshape(1, channels), pltpu.HBM),
    )


def correlate_kernel(windows, samples, lag_dev, ext_ref, out_ref, wide):
    group = pl.program_id(0)
    first_lag = lax.axis_index("tm") * lag_dev - LAG
    norm_scale = 1.0 / math.sqrt(samples * windows)
    rows = ext_ref.shape[0]

    @pl.when(group == 0)
    def _():
        wide[0:rows, :] = ext_ref[...]
        wide[rows:, :] = jnp.zeros((wide.shape[0] - rows, wide.shape[1]), wide.dtype)

    base = pl.multiple_of(group * SUB, SUB)
    own = wide[pl.ds(base, SUB), :].astype(jnp.float32)
    partners = wide[pl.ds(base, OFF), :]
    beyond = wide[pl.ds(pl.multiple_of(base + OFF, SUB), LANES), :]
    lag = first_lag + lax.broadcasted_iota(jnp.int32, (lag_dev, samples), 0)
    at = lax.broadcasted_iota(jnp.int32, (lag_dev, samples), 1) - lag
    keep = (at >= 0) & (at < samples)
    lane = lax.broadcasted_iota(jnp.int32, (lag_dev, LANES), 1)
    if lag_dev % samples == 0 and LAG % samples == 0:
        turn = None
    else:
        turn = lax.rem(first_lag + samples * (-(-LAG // samples)), samples)
    blocks = []
    for r in range(SUB):
        parts = []
        for w in range(windows):
            trace = own[r : r + 1, w * samples : (w + 1) * samples]
            if turn is not None:
                trace = pltpu.roll(jnp.broadcast_to(trace, (8, samples)), turn, 1)[0:1]
            trace = jnp.broadcast_to(trace, (lag_dev, samples))
            rolled = pltpu.roll(trace, 0, 1, stride=1, stride_axis=0)
            parts.append(jnp.where(keep, rolled, 0.0).astype(jnp.bfloat16))
        blocks.append(jnp.concatenate(parts, axis=1))
    toeplitz = jnp.concatenate(blocks, axis=0)
    contract = (((1,), (1,)), ((), ()))
    near = lax.dot_general(toeplitz, partners, contract, preferred_element_type=jnp.float32)
    far = lax.dot_general(toeplitz, beyond, contract, preferred_element_type=jnp.float32)
    for r in range(SUB):
        first = r * lag_dev
        skip = r + 1
        columns = [
            near[first : first + lag_dev, k * LANES : (k + 1) * LANES] for k in range(OFF // LANES)
        ]
        columns[0] = jnp.where(lane < skip, far[first : first + lag_dev], columns[0])
        columns = [(c * norm_scale).astype(jnp.bfloat16).astype(jnp.float32) for c in columns]
        turned = [pltpu.roll(column, LANES - skip, 1) for column in columns]
        for k in range(len(columns)):
            following = turned[(k + 1) % len(columns)]
            value = jnp.where(lane < LANES - skip, turned[k], following)
            out_ref[r, :, k * LANES : (k + 1) * LANES] = value.astype(jnp.bfloat16)


def correlate(extended, channels, windows, lag_dev):
    depth = extended.shape[1]
    samples = depth // windows
    return pl.pallas_call(
        functools.partial(correlate_kernel, windows, samples, lag_dev),
        out_shape=jax.ShapeDtypeStruct((channels, lag_dev, OFF), jnp.bfloat16),
        grid=(channels // SUB,),
        in_specs=[pl.BlockSpec(extended.shape, lambda g: (0, 0))],
        out_specs=pl.BlockSpec((SUB, lag_dev, OFF), lambda g: (g, 0, 0)),
        scratch_shapes=[pltpu.VMEM((channels - SUB + OFF + LANES, depth), jnp.bfloat16)],
        compiler_params=pltpu.CompilerParams(vmem_limit_bytes=VMEM_GRANT),
        name="correlate",
    )(extended)


def sweep_kernel(windows, samples, traces, plane, out_ref, staged, ship_sem):
    positive = lax.axis_index("tm")
    channels, lag_dev, _ = staged.shape
    pad = samples - SUB
    lane = lax.broadcasted_iota(jnp.int32, (SUB, LANES), 1)
    half = SUB // 2
    groups = channels // (2 * SUB)
    steps = lag_dev // (2 * SUB) * groups

    def place(turn):
        step, odd = divmod(turn, 2)
        return (2 * (step % groups) + odd) * SUB, 2 * (step // groups)

    def weights(turn, band, first_lane, count):
        channel, low = place(turn)
        start = pl.multiple_of((low + band) * SUB + positive * pad, SUB)
        lanes = channel // LANES * LANES + first_lane
        return jnp.concatenate(
            [plane[w, pl.ds(start, samples), lanes : lanes + count] for w in range(windows)], axis=0
        )

    def finish(turn, accs, i):
        channel, low = place(turn)
        part, k = divmod(i, half)
        near = [pltpu.matmul_pop(accs[turn % 2][unit][part][k]) for unit in range(2)]
        far = pltpu.matmul_pop(accs[turn % 2][part][2][k])
        skip = (channel + i) % LANES + 1
        for band in range(2):
            columns = [
                near[band][:, :LANES],
                near[band][:, LANES:],
                far[:, band * LANES : (band + 1) * LANES],
            ]
            values = [
                pltpu.roll(jnp.where(lane < skip, columns[k + 1], columns[k]), LANES - skip, 1)
                for k in range(2)
            ]
            first = (low + band) * SUB
            staged[channel + i, first : first + SUB, :] = jnp.concatenate(values, axis=1).astype(
                jnp.bfloat16
            )

    def launch(turn, accs):
        channel, _ = place(turn)
        odd = turn % 2
        if not odd:
            for unit in range(2):
                pltpu.matmul_push_rhs(weights(turn, unit, 0, OFF), 0, unit)
        count = done = 0
        for kind in (2, 0, 1) if odd else (0, 1, 2):
            for i in range(half):
                staged_rhs = None
                if i == 0 and kind == 0:
                    staged_rhs = 0
                elif i == 0 and kind == 2 and not odd:
                    staged_rhs = 1
                for unit in range(2):
                    part = unit if kind == 2 else kind
                    pltpu.matmul_acc_lhs(
                        accs[odd][unit][kind][i],
                        traces[channel + part * half + i],
                        load_staged_rhs=staged_rhs,
                    )
                if i == 0 and kind == 0 and not odd:
                    for unit in range(2):
                        far = [weights(turn, band, OFF, LANES) for band in range(2)]
                        pltpu.matmul_push_rhs(jnp.concatenate(far, axis=1), 1, unit)
                if i == 0 and kind == 2 and odd:
                    for unit in range(2):
                        pltpu.matmul_push_rhs(weights(turn, unit, 0, OFF), 0, unit)
                count += 1
                while turn and done < SUB * count // (3 * half):
                    finish(turn - 1, accs, done)
                    done += 1

    def ship(turn):
        channel, low = place(turn)
        where = (pl.ds(channel, SUB), pl.ds(low * SUB, 2 * SUB), slice(None))
        return pltpu.make_async_copy(staged.at[where], out_ref.at[where], ship_sem.at[turn])

    def run(*flat):
        flat = iter(flat)
        accs = [[[None] * 3 for _ in range(2)] for _ in range(2)]
        for odd in range(2):
            for unit in range(2):
                for kind in range(3):
                    accs[odd][unit][kind] = [next(flat) for _ in range(half)]
        for turn in range(2 * steps):
            launch(turn, accs)
            if turn:
                ship(turn - 1).start()
        for i in range(SUB):
            finish(2 * steps - 1, accs, i)
        ship(2 * steps - 1).start()

    pl.run_scoped(
        run,
        *[
            pltpu.ACC(unit)((SUB, OFF), jnp.float32)
            for odd in range(2)
            for unit in range(2)
            for _ in range(3 * half)
        ],
    )
    for turn in range(2 * steps):
        ship(turn).wait()


def sweep(traces, plane, lag_dev):
    channels, _, depth = traces.shape
    windows = plane.shape[0]
    turns = lag_dev // (2 * SUB) * (channels // SUB)
    vmem = pl.BlockSpec(memory_space=pltpu.VMEM)
    return pl.pallas_call(
        functools.partial(sweep_kernel, windows, depth // windows),
        out_shape=jax.ShapeDtypeStruct((channels, lag_dev, OFF), jnp.bfloat16),
        in_specs=[vmem, vmem],
        out_specs=pl.BlockSpec(memory_space=pltpu.HBM),
        scratch_shapes=[
            pltpu.VMEM((channels, lag_dev, OFF), jnp.bfloat16),
            pltpu.SemaphoreType.DMA((turns,)),
        ],
        compiler_params=pltpu.CompilerParams(vmem_limit_bytes=VMEM_GRANT),
        name="sweep",
    )(traces, plane)


def shards(raw_strain, fir_taps, live_mask):
    n_chan = lax.axis_size("chan")
    n_tm = lax.axis_size("tm")
    channels = live_mask.shape[0]
    lag_dev = 2 * LAG // n_tm
    samples = raw_strain.shape[2] * n_chan // STRIDE
    swept = n_tm == 2 and samples == LAG == LANES and 2 * samples == OFF
    swept = swept and channels % (2 * SUB) == 0 and channels <= STAGED_CHANNELS
    prepared = prepare(raw_strain, fir_taps, live_mask, n_chan, n_tm, swept)
    if swept:
        return sweep(*prepared, lag_dev)
    return correlate(*prepared, channels, n_tm, lag_dev)


def solution(mesh):
    placed = (P("tm", "fibre", "chan"), P(), P(("fibre", "chan")))
    return jax.shard_map(
        shards,
        mesh=mesh,
        in_specs=placed,
        out_specs=P(("fibre", "chan"), "tm", None),
        check_vma=False,
    )
```

```python
import functools
import math

import jax
import jax.numpy as jnp
from jax import lax
from jax.experimental import pallas as pl
from jax.experimental.pallas import tpu as pltpu
from jax.sharding import PartitionSpec as P

OFF = 256
LAG = 128
TAPS = 64
STRIDE = 4
HIST = 60
LANES = 128
SUB = 16
STAGED_CHANNELS = 256
VMEM_GRANT = 28 * 2**20
MESH = pl.DeviceIdType.MESH


def tap_block(taps_row, member, members, tract_len, rows):
    width = members * tract_len
    tap = lax.broadcasted_iota(jnp.int32, (TAPS, width), 0)
    lane = lax.broadcasted_iota(jnp.int32, (TAPS, width), 1)
    flip = jnp.where(tap + lane == TAPS - 1, 1.0, 0.0).astype(jnp.bfloat16)
    reversed_row = jnp.dot(
        jnp.broadcast_to(taps_row, (8, TAPS)), flip, preferred_element_type=jnp.float32
    )[0:1]
    start = (member * tract_len - HIST) % width
    rolled = pltpu.roll(
        jnp.broadcast_to(reversed_row, (rows, width)), start, 1, stride=STRIDE, stride_axis=0
    )
    row = lax.broadcasted_iota(jnp.int32, (rows, width), 0)
    local = lax.broadcasted_iota(jnp.int32, (rows, width), 1) - member * tract_len
    index = STRIDE * row + STRIDE - 1 - local
    keep = (local >= 0) & (local < tract_len) & (index >= 0) & (index < TAPS)
    return jnp.where(keep, rolled, 0.0).astype(jnp.bfloat16)


def prepare_kernel(
    n_chan,
    n_tm,
    members,
    outs,
    raw_hbm,
    taps_hbm,
    mask_hbm,
    *refs,
):
    out_refs, refs = refs[:outs], refs[outs:]
    (
        raw_ref,
        taps_ref,
        mask_ref,
        packed,
        received,
        fir,
        fir_turned,
        white,
        extended,
        send_a,
        recv_a,
        send_b,
        recv_b,
        load,
    ) = refs
    loads = [
        pltpu.make_async_copy(source, target, load.at[i])
        for i, (source, target) in enumerate(
            [(raw_hbm, raw_ref), (taps_hbm, taps_ref), (mask_hbm, mask_ref)]
        )
    ]
    for copy in loads:
        copy.start()
    me = lax.axis_index("chan")
    my_tm = lax.axis_index("tm")
    tract_len = raw_hbm.shape[1]
    channels, samples = white.shape
    part = channels // members
    width = members * tract_len
    outputs = tract_len // STRIDE
    reach = -(-OFF // channels)

    def signal(chan, turn):
        pl.semaphore_signal(
            barrier,
            inc=1,
            device_id={"chan": chan, "tm": lax.rem(my_tm + turn, n_tm)},
            device_id_type=MESH,
        )

    barrier = pltpu.get_barrier_semaphore()
    for step in range(1, n_chan):
        signal(lax.rem(me + step, n_chan), 0)
    for turn in range(1, n_tm):
        signal(me, turn)
        for k in range(1, reach + 1):

            @pl.when(me >= k)
            def _():
                signal(me - k, turn)

            @pl.when(me + k < n_chan)
            def _():
                signal(me + k, turn)

    loads[0].wait()
    turned = raw_ref[0].astype(jnp.float32).T.astype(jnp.bfloat16)
    for block in range(n_chan):
        first = block * channels
        pieces = [turned[first + m * part : first + (m + 1) * part] for m in range(members)]
        packed[block] = jnp.concatenate(pieces, axis=1)
    near_blocks = 1
    for k in range(1, reach + 1):
        near_blocks = near_blocks + (me + n_chan - k) // n_chan + 1 - (me + k) // n_chan
    pl.semaphore_wait(barrier, n_chan - 1 + (n_tm - 1) * near_blocks)

    def spread(target, slot):
        return pltpu.make_async_remote_copy(
            src_ref=packed.at[target],
            dst_ref=received.at[me],
            send_sem=send_a.at[slot],
            recv_sem=recv_a.at[me],
            device_id={"chan": target},
            device_id_type=MESH,
        )

    ways = [(distance, side) for distance in range(n_chan - 1, 0, -1) for side in range(2)]
    for distance, side in ways:
        target = me + distance if side else me - distance

        @pl.when(target < n_chan if side else target >= 0)
        def _():
            spread(target, 2 * distance + side).start()

    received[me] = packed[me]
    loads[1].wait()
    loads[2].wait()
    fir[...] = jnp.zeros_like(fir)
    taps_row = taps_ref[...]
    rows = 2 * outputs
    for m in range(members):
        block = tap_block(taps_row, m, members, tract_len, rows)
        for source in range(n_chan):
            first = m * samples + source * outputs
            count = min(rows, samples - source * outputs)
            fir[first : first + count, source * width : (source + 1) * width] = block[:count]
    fir_turned[...] = fir[...].astype(jnp.float32).T.astype(jnp.bfloat16)
    alive = mask_ref[...].astype(jnp.float32)
    diagonal = lax.broadcasted_iota(jnp.int32, (channels, channels), 0) == lax.broadcasted_iota(
        jnp.int32, (channels, channels), 1
    )
    alive_column = jnp.sum(
        jnp.where(diagonal, jnp.broadcast_to(alive, (channels, channels)), 0.0),
        axis=1,
        keepdims=True,
    )

    for k in range(1, reach + 1):
        count = min(channels, OFF - (k - 1) * channels)

        @pl.when(me + k >= n_chan)
        def _():
            extended[k * channels : k * channels + count, :] = jnp.zeros(
                (count, extended.shape[1]), extended.dtype
            )

    if len(out_refs) > 1:
        traces, plane = out_refs
        pad = samples - SUB
        for w in range(n_tm):
            plane[w, 0:pad, :] = jnp.zeros((pad, plane.shape[2]), plane.dtype)
            plane[w, pad + samples :, :] = jnp.zeros((pad, plane.shape[2]), plane.dtype)
        tail = extended.shape[0] - channels - OFF
        if tail:
            extended[channels + OFF :, :] = jnp.zeros((tail, extended.shape[1]), extended.dtype)

    for source in range(n_chan):

        @pl.when(me != source)
        def _():
            pltpu.make_async_remote_copy(
                src_ref=packed.at[source],
                dst_ref=received.at[source],
                send_sem=send_a.at[0],
                recv_sem=recv_a.at[source],
                device_id={"chan": source},
                device_id_type=MESH,
            ).wait_recv()

    tracts = jnp.concatenate([received[d] for d in range(n_chan)], axis=1)
    filtered = jnp.dot(tracts, fir_turned[...], preferred_element_type=jnp.float32)
    for m in range(members):
        decimated = filtered[:, m * samples : (m + 1) * samples]
        decimated = decimated.astype(jnp.bfloat16).astype(jnp.float32)
        loudness = jnp.sqrt(jnp.mean(decimated * decimated, axis=1, keepdims=True) + 1e-06)
        gain = alive_column[m * part : (m + 1) * part] / loudness
        white[m * part : (m + 1) * part, :] = (decimated * gain).astype(jnp.bfloat16)

    def share(k, turn):
        count = channels if k == 0 else min(channels, OFF - (k - 1) * channels)
        window = pl.multiple_of(my_tm * samples, LANES)
        return pltpu.make_async_remote_copy(
            src_ref=white.at[pl.ds(0, count), :],
            dst_ref=extended.at[pl.ds(k * channels, count), pl.ds(window, samples)],
            send_sem=send_b.at[k, turn],
            recv_sem=recv_b.at[k, turn],
            device_id={"chan": me - k, "tm": lax.rem(my_tm + turn, n_tm)},
            device_id_type=MESH,
        )

    pairs = [(0, t) for t in range(1, n_tm)]
    pairs += [(k, t) for t in range(n_tm - 1, -1, -1) for k in range(reach, 0, -1)]
    for k, turn in pairs:

        @pl.when(me >= k)
        def _():
            share(k, turn).start()

    own = pl.multiple_of(my_tm * samples, LANES)
    extended[0:channels, pl.ds(own, samples)] = white[...]
    if len(out_refs) > 1:
        traces, plane = out_refs
        lay_rows(white[...], traces, own, my_tm, n_tm)
    tiles = extended.shape[0] // LANES
    laid = 0
    for k in range(reach + 1):
        for turn in range(n_tm):
            if k == 0 and turn == 0:
                continue

            @pl.when(me + k < n_chan)
            def _():
                share(k, turn).wait_recv()

        if len(out_refs) == 1:
            continue
        if k == 0:
            for turn in range(1, n_tm):
                window = lax.rem(my_tm + n_tm - turn, n_tm)
                lanes = pl.multiple_of(window * samples, LANES)
                lay_rows(extended[0:channels, pl.ds(lanes, samples)], traces, lanes, my_tm, n_tm)
        ready = tiles if k == reach else (k + 1) * channels // LANES
        for tile in range(laid, ready):
            lanes = slice(tile * LANES, (tile + 1) * LANES)
            turned = extended[lanes, :].astype(jnp.float32).T.astype(jnp.bfloat16)
            for w in range(n_tm):
                plane[w, samples - SUB : 2 * samples - SUB, lanes] = turned[
                    w * samples : (w + 1) * samples
                ]
        laid = ready

    for distance, side in ways:
        target = me + distance if side else me - distance

        @pl.when(target < n_chan if side else target >= 0)
        def _():
            spread(target, 2 * distance + side).wait_send()

    for k, turn in pairs:

        @pl.when(me >= k)
        def _():
            share(k, turn).wait_send()

    if len(out_refs) == 1:
        out_refs[0][...] = extended[...]


def lay_rows(own, traces, lanes, my_tm, n_tm):
    channels, samples = own.shape
    positive = my_tm
    scale = 1.0 / math.sqrt(samples * n_tm)
    row = lax.broadcasted_iota(jnp.int32, (SUB, samples), 0)
    at = lax.broadcasted_iota(jnp.int32, (SUB, samples), 1) - row + SUB * (1 - positive)
    weight = jnp.where((at >= 0) & (at < samples), scale, 0.0)
    moved = pltpu.roll(own.astype(jnp.float32), (1 - positive) * (samples - SUB), 1)
    for channel in range(channels):
        trace = jnp.broadcast_to(moved[channel : channel + 1], (SUB, samples))
        rolled = pltpu.roll(trace, 0, 1, stride=1, stride_axis=0)
        traces[channel, :, pl.ds(lanes, samples)] = (rolled * weight).astype(jnp.bfloat16)


def prepare(raw_strain, fir_taps, live_mask, n_chan, n_tm, swept):
    _, all_channels, tract_len = raw_strain.shape
    channels = all_channels // n_chan
    samples = tract_len * n_chan // STRIDE
    members = max(1, LANES // tract_len)
    part = channels // members
    width = members * tract_len
    reach = -(-OFF // channels)
    vmem = pl.BlockSpec(memory_space=pltpu.VMEM)
    hbm = pl.BlockSpec(memory_space=pltpu.HBM)
    landing = channels + OFF
    outs = [(landing, n_tm * samples)]
    if swept:
        landing = -(-landing // LANES) * LANES
        outs = [
            (channels, SUB, n_tm * samples),
            (n_tm, 3 * samples - 2 * SUB, landing),
        ]
    return pl.pallas_call(
        functools.partial(prepare_kernel, n_chan, n_tm, members, len(outs)),
        out_shape=[jax.ShapeDtypeStruct(shape, jnp.bfloat16) for shape in outs],
        in_specs=[hbm, hbm, hbm],
        out_specs=[vmem] * len(outs),
        scratch_shapes=[
            pltpu.VMEM((1, tract_len, all_channels), jnp.bfloat16),
            pltpu.VMEM((1, TAPS), jnp.bfloat16),
            pltpu.VMEM((1, channels), jnp.int32),
            pltpu.VMEM((n_chan, part, width), jnp.bfloat16),
            pltpu.VMEM((n_chan, part, width), jnp.bfloat16),
            pltpu.VMEM((members * samples, n_chan * width), jnp.bfloat16),
            pltpu.VMEM((n_chan * width, members * samples), jnp.bfloat16),
            pltpu.VMEM((channels, samples), jnp.bfloat16),
            pltpu.VMEM((landing, n_tm * samples), jnp.bfloat16),
            pltpu.SemaphoreType.DMA((2 * n_chan,)),
            pltpu.SemaphoreType.DMA((n_chan,)),
            pltpu.SemaphoreType.DMA((reach + 1, n_tm)),
            pltpu.SemaphoreType.DMA((reach + 1, n_tm)),
            pltpu.SemaphoreType.DMA((3,)),
        ],
        compiler_params=pltpu.CompilerParams(
            collective_id=0, has_side_effects=True, vmem_limit_bytes=VMEM_GRANT
        ),
        name="prepare",
    )(
        pltpu.with_memory_space_constraint(raw_strain.transpose(0, 2, 1), pltpu.HBM),
        pltpu.with_memory_space_constraint(fir_taps.reshape(1, TAPS), pltpu.HBM),
        pltpu.with_memory_space_constraint(live_mask.reshape(1, channels), pltpu.HBM),
    )


def correlate_kernel(windows, samples, lag_dev, ext_ref, out_ref, wide):
    group = pl.program_id(0)
    first_lag = lax.axis_index("tm") * lag_dev - LAG
    norm_scale = 1.0 / math.sqrt(samples * windows)
    rows = ext_ref.shape[0]

    @pl.when(group == 0)
    def _():
        wide[0:rows, :] = ext_ref[...]
        wide[rows:, :] = jnp.zeros((wide.shape[0] - rows, wide.shape[1]), wide.dtype)

    base = pl.multiple_of(group * SUB, SUB)
    own = wide[pl.ds(base, SUB), :].astype(jnp.float32)
    partners = wide[pl.ds(base, OFF), :]
    beyond = wide[pl.ds(pl.multiple_of(base + OFF, SUB), LANES), :]
    lag = first_lag + lax.broadcasted_iota(jnp.int32, (lag_dev, samples), 0)
    at = lax.broadcasted_iota(jnp.int32, (lag_dev, samples), 1) - lag
    keep = (at >= 0) & (at < samples)
    lane = lax.broadcasted_iota(jnp.int32, (lag_dev, LANES), 1)
    if lag_dev % samples == 0 and LAG % samples == 0:
        turn = None
    else:
        turn = lax.rem(first_lag + samples * (-(-LAG // samples)), samples)
    blocks = []
    for r in range(SUB):
        parts = []
        for w in range(windows):
            trace = own[r : r + 1, w * samples : (w + 1) * samples]
            if turn is not None:
                trace = pltpu.roll(jnp.broadcast_to(trace, (8, samples)), turn, 1)[0:1]
            trace = jnp.broadcast_to(trace, (lag_dev, samples))
            rolled = pltpu.roll(trace, 0, 1, stride=1, stride_axis=0)
            parts.append(jnp.where(keep, rolled, 0.0).astype(jnp.bfloat16))
        blocks.append(jnp.concatenate(parts, axis=1))
    toeplitz = jnp.concatenate(blocks, axis=0)
    contract = (((1,), (1,)), ((), ()))
    near = lax.dot_general(toeplitz, partners, contract, preferred_element_type=jnp.float32)
    far = lax.dot_general(toeplitz, beyond, contract, preferred_element_type=jnp.float32)
    for r in range(SUB):
        first = r * lag_dev
        skip = r + 1
        columns = [
            near[first : first + lag_dev, k * LANES : (k + 1) * LANES] for k in range(OFF // LANES)
        ]
        columns[0] = jnp.where(lane < skip, far[first : first + lag_dev], columns[0])
        columns = [(c * norm_scale).astype(jnp.bfloat16).astype(jnp.float32) for c in columns]
        turned = [pltpu.roll(column, LANES - skip, 1) for column in columns]
        for k in range(len(columns)):
            following = turned[(k + 1) % len(columns)]
            value = jnp.where(lane < LANES - skip, turned[k], following)
            out_ref[r, :, k * LANES : (k + 1) * LANES] = value.astype(jnp.bfloat16)


def correlate(extended, channels, windows, lag_dev):
    depth = extended.shape[1]
    samples = depth // windows
    return pl.pallas_call(
        functools.partial(correlate_kernel, windows, samples, lag_dev),
        out_shape=jax.ShapeDtypeStruct((channels, lag_dev, OFF), jnp.bfloat16),
        grid=(channels // SUB,),
        in_specs=[pl.BlockSpec(extended.shape, lambda g: (0, 0))],
        out_specs=pl.BlockSpec((SUB, lag_dev, OFF), lambda g: (g, 0, 0)),
        scratch_shapes=[pltpu.VMEM((channels - SUB + OFF + LANES, depth), jnp.bfloat16)],
        compiler_params=pltpu.CompilerParams(vmem_limit_bytes=VMEM_GRANT),
        name="correlate",
    )(extended)


def sweep_kernel(windows, samples, traces, plane, out_ref, staged, ship_sem):
    positive = lax.axis_index("tm")
    channels, lag_dev, _ = staged.shape
    pad = samples - SUB
    lane = lax.broadcasted_iota(jnp.int32, (SUB, LANES), 1)
    half = SUB // 2
    groups = channels // (2 * SUB)
    steps = lag_dev // (2 * SUB) * groups

    def place(turn):
        step, odd = divmod(turn, 2)
        return (2 * (step % groups) + odd) * SUB, 2 * (step // groups)

    def weights(turn, band, first_lane, count):
        channel, low = place(turn)
        start = pl.multiple_of((low + band) * SUB + positive * pad, SUB)
        lanes = channel // LANES * LANES + first_lane
        return jnp.concatenate(
            [plane[w, pl.ds(start, samples), lanes : lanes + count] for w in range(windows)], axis=0
        )

    def finish(turn, accs, i):
        channel, low = place(turn)
        part, k = divmod(i, half)
        near = [pltpu.matmul_pop(accs[turn % 2][unit][part][k]) for unit in range(2)]
        far = pltpu.matmul_pop(accs[turn % 2][part][2][k])
        skip = (channel + i) % LANES + 1
        for band in range(2):
            columns = [
                near[band][:, :LANES],
                near[band][:, LANES:],
                far[:, band * LANES : (band + 1) * LANES],
            ]
            values = [
                pltpu.roll(jnp.where(lane < skip, columns[k + 1], columns[k]), LANES - skip, 1)
                for k in range(2)
            ]
            first = (low + band) * SUB
            staged[channel + i, first : first + SUB, :] = jnp.concatenate(values, axis=1).astype(
                jnp.bfloat16
            )

    def launch(turn, accs):
        channel, _ = place(turn)
        odd = turn % 2
        if not odd:
            for unit in range(2):
                pltpu.matmul_push_rhs(weights(turn, unit, 0, OFF), 0, unit)
        count = done = 0
        for kind in (2, 0, 1) if odd else (0, 1, 2):
            for i in range(half):
                staged_rhs = None
                if i == 0 and kind == 0:
                    staged_rhs = 0
                elif i == 0 and kind == 2 and not odd:
                    staged_rhs = 1
                for unit in range(2):
                    part = unit if kind == 2 else kind
                    pltpu.matmul_acc_lhs(
                        accs[odd][unit][kind][i],
                        traces[channel + part * half + i],
                        load_staged_rhs=staged_rhs,
                    )
                if i == 0 and kind == 0 and not odd:
                    for unit in range(2):
                        far = [weights(turn, band, OFF, LANES) for band in range(2)]
                        pltpu.matmul_push_rhs(jnp.concatenate(far, axis=1), 1, unit)
                if i == 0 and kind == 2 and odd:
                    for unit in range(2):
                        pltpu.matmul_push_rhs(weights(turn, unit, 0, OFF), 0, unit)
                count += 1
                while turn and done < SUB * count // (3 * half):
                    finish(turn - 1, accs, done)
                    done += 1

    def ship(turn):
        channel, low = place(turn)
        where = (pl.ds(channel, SUB), pl.ds(low * SUB, 2 * SUB), slice(None))
        return pltpu.make_async_copy(staged.at[where], out_ref.at[where], ship_sem.at[turn])

    def run(*flat):
        flat = iter(flat)
        accs = [[[None] * 3 for _ in range(2)] for _ in range(2)]
        for odd in range(2):
            for unit in range(2):
                for kind in range(3):
                    accs[odd][unit][kind] = [next(flat) for _ in range(half)]
        for turn in range(2 * steps):
            launch(turn, accs)
            if turn:
                ship(turn - 1).start()
        for i in range(SUB):
            finish(2 * steps - 1, accs, i)
        ship(2 * steps - 1).start()

    pl.run_scoped(
        run,
        *[
            pltpu.ACC(unit)((SUB, OFF), jnp.float32)
            for odd in range(2)
            for unit in range(2)
            for _ in range(3 * half)
        ],
    )
    for turn in range(2 * steps):
        ship(turn).wait()


def sweep(traces, plane, lag_dev):
    channels, _, depth = traces.shape
    windows = plane.shape[0]
    turns = lag_dev // (2 * SUB) * (channels // SUB)
    vmem = pl.BlockSpec(memory_space=pltpu.VMEM)
    return pl.pallas_call(
        functools.partial(sweep_kernel, windows, depth // windows),
        out_shape=jax.ShapeDtypeStruct((channels, lag_dev, OFF), jnp.bfloat16),
        in_specs=[vmem, vmem],
        out_specs=pl.BlockSpec(memory_space=pltpu.HBM),
        scratch_shapes=[
            pltpu.VMEM((channels, lag_dev, OFF), jnp.bfloat16),
            pltpu.SemaphoreType.DMA((turns,)),
        ],
        compiler_params=pltpu.CompilerParams(vmem_limit_bytes=VMEM_GRANT),
        name="sweep",
    )(traces, plane)


def shards(raw_strain, fir_taps, live_mask):
    n_chan = lax.axis_size("chan")
    n_tm = lax.axis_size("tm")
    channels = live_mask.shape[0]
    lag_dev = 2 * LAG // n_tm
    samples = raw_strain.shape[2] * n_chan // STRIDE
    swept = n_tm == 2 and samples == LAG == LANES and 2 * samples == OFF
    swept = swept and channels % (2 * SUB) == 0 and channels <= STAGED_CHANNELS
    prepared = prepare(raw_strain, fir_taps, live_mask, n_chan, n_tm, swept)
    if swept:
        return sweep(*prepared, lag_dev)
    return correlate(*prepared, channels, n_tm, lag_dev)


def solution(mesh):
    placed = (P("tm", "fibre", "chan"), P(), P(("fibre", "chan")))
    return jax.shard_map(
        shards,
        mesh=mesh,
        in_specs=placed,
        out_specs=P(("fibre", "chan"), "tm", None),
        check_vma=False,
    )
```

```python
import functools
import math

import jax
import jax.numpy as jnp
from jax import lax
from jax.experimental import pallas as pl
from jax.experimental.pallas import tpu as pltpu
from jax.sharding import PartitionSpec as P

OFF = 256
LAG = 128
TAPS = 64
STRIDE = 4
HIST = 60
LANES = 128
SUB = 16
STAGED_CHANNELS = 256
VMEM_GRANT = 28 * 2**20
MESH = pl.DeviceIdType.MESH


def tap_block(taps_row, member, members, tract_len, rows):
    width = members * tract_len
    tap = lax.broadcasted_iota(jnp.int32, (TAPS, width), 0)
    lane = lax.broadcasted_iota(jnp.int32, (TAPS, width), 1)
    flip = jnp.where(tap + lane == TAPS - 1, 1.0, 0.0).astype(jnp.bfloat16)
    reversed_row = jnp.dot(
        jnp.broadcast_to(taps_row, (8, TAPS)), flip, preferred_element_type=jnp.float32
    )[0:1]
    start = (member * tract_len - HIST) % width
    rolled = pltpu.roll(
        jnp.broadcast_to(reversed_row, (rows, width)), start, 1, stride=STRIDE, stride_axis=0
    )
    row = lax.broadcasted_iota(jnp.int32, (rows, width), 0)
    local = lax.broadcasted_iota(jnp.int32, (rows, width), 1) - member * tract_len
    index = STRIDE * row + STRIDE - 1 - local
    keep = (local >= 0) & (local < tract_len) & (index >= 0) & (index < TAPS)
    return jnp.where(keep, rolled, 0.0).astype(jnp.bfloat16)


def prepare_kernel(
    n_chan,
    n_tm,
    members,
    outs,
    raw_hbm,
    taps_hbm,
    mask_hbm,
    *refs,
):
    out_refs, refs = refs[:outs], refs[outs:]
    (
        raw_ref,
        taps_ref,
        mask_ref,
        packed,
        received,
        fir,
        fir_turned,
        white,
        extended,
        send_a,
        recv_a,
        send_b,
        recv_b,
        load,
    ) = refs
    loads = [
        pltpu.make_async_copy(source, target, load.at[i])
        for i, (source, target) in enumerate(
            [(raw_hbm, raw_ref), (taps_hbm, taps_ref), (mask_hbm, mask_ref)]
        )
    ]
    for copy in loads:
        copy.start()
    me = lax.axis_index("chan")
    my_tm = lax.axis_index("tm")
    tract_len = raw_hbm.shape[1]
    channels, samples = white.shape
    part = channels // members
    width = members * tract_len
    outputs = tract_len // STRIDE
    reach = -(-OFF // channels)

    def signal(chan, turn):
        pl.semaphore_signal(
            barrier,
            inc=1,
            device_id={"chan": chan, "tm": lax.rem(my_tm + turn, n_tm)},
            device_id_type=MESH,
        )

    barrier = pltpu.get_barrier_semaphore()
    for step in range(1, n_chan):
        signal(lax.rem(me + step, n_chan), 0)
    for turn in range(1, n_tm):
        signal(me, turn)
        for k in range(1, reach + 1):

            @pl.when(me >= k)
            def _():
                signal(me - k, turn)

            @pl.when(me + k < n_chan)
            def _():
                signal(me + k, turn)

    loads[0].wait()
    turned = raw_ref[0].astype(jnp.float32).T.astype(jnp.bfloat16)
    for block in range(n_chan):
        first = block * channels
        pieces = [turned[first + m * part : first + (m + 1) * part] for m in range(members)]
        packed[block] = jnp.concatenate(pieces, axis=1)
    near_blocks = 1
    for k in range(1, reach + 1):
        near_blocks = near_blocks + (me + n_chan - k) // n_chan + 1 - (me + k) // n_chan
    pl.semaphore_wait(barrier, n_chan - 1 + (n_tm - 1) * near_blocks)

    def spread(step):
        target = lax.rem(me + step, n_chan)
        return pltpu.make_async_remote_copy(
            src_ref=packed.at[target],
            dst_ref=received.at[me],
            send_sem=send_a.at[step],
            recv_sem=recv_a.at[me],
            device_id={"chan": target},
            device_id_type=MESH,
        )

    for step in range(n_chan - 1, 0, -1):
        spread(step).start()

    received[me] = packed[me]
    loads[1].wait()
    loads[2].wait()
    fir[...] = jnp.zeros_like(fir)
    taps_row = taps_ref[...]
    rows = 2 * outputs
    for m in range(members):
        block = tap_block(taps_row, m, members, tract_len, rows)
        for source in range(n_chan):
            first = m * samples + source * outputs
            count = min(rows, samples - source * outputs)
            fir[first : first + count, source * width : (source + 1) * width] = block[:count]
    fir_turned[...] = fir[...].astype(jnp.float32).T.astype(jnp.bfloat16)
    alive = mask_ref[...].astype(jnp.float32)
    diagonal = lax.broadcasted_iota(jnp.int32, (channels, channels), 0) == lax.broadcasted_iota(
        jnp.int32, (channels, channels), 1
    )
    alive_column = jnp.sum(
        jnp.where(diagonal, jnp.broadcast_to(alive, (channels, channels)), 0.0),
        axis=1,
        keepdims=True,
    )

    for k in range(1, reach + 1):
        count = min(channels, OFF - (k - 1) * channels)

        @pl.when(me + k >= n_chan)
        def _():
            extended[k * channels : k * channels + count, :] = jnp.zeros(
                (count, extended.shape[1]), extended.dtype
            )

    if len(out_refs) > 1:
        traces, plane = out_refs
        pad = samples - SUB
        for w in range(n_tm):
            plane[w, 0:pad, :] = jnp.zeros((pad, plane.shape[2]), plane.dtype)
            plane[w, pad + samples :, :] = jnp.zeros((pad, plane.shape[2]), plane.dtype)
        tail = extended.shape[0] - channels - OFF
        if tail:
            extended[channels + OFF :, :] = jnp.zeros((tail, extended.shape[1]), extended.dtype)

    for step in range(1, n_chan):
        source = lax.rem(me + step, n_chan)
        pltpu.make_async_remote_copy(
            src_ref=packed.at[source],
            dst_ref=received.at[source],
            send_sem=send_a.at[step],
            recv_sem=recv_a.at[source],
            device_id={"chan": source},
            device_id_type=MESH,
        ).wait_recv()

    tracts = jnp.concatenate([received[d] for d in range(n_chan)], axis=1)
    filtered = jnp.dot(tracts, fir_turned[...], preferred_element_type=jnp.float32)
    for m in range(members):
        decimated = filtered[:, m * samples : (m + 1) * samples]
        decimated = decimated.astype(jnp.bfloat16).astype(jnp.float32)
        loudness = jnp.sqrt(jnp.mean(decimated * decimated, axis=1, keepdims=True) + 1e-06)
        gain = alive_column[m * part : (m + 1) * part] / loudness
        white[m * part : (m + 1) * part, :] = (decimated * gain).astype(jnp.bfloat16)

    def share(k, turn):
        count = channels if k == 0 else min(channels, OFF - (k - 1) * channels)
        window = pl.multiple_of(my_tm * samples, LANES)
        return pltpu.make_async_remote_copy(
            src_ref=white.at[pl.ds(0, count), :],
            dst_ref=extended.at[pl.ds(k * channels, count), pl.ds(window, samples)],
            send_sem=send_b.at[k, turn],
            recv_sem=recv_b.at[k, turn],
            device_id={"chan": me - k, "tm": lax.rem(my_tm + turn, n_tm)},
            device_id_type=MESH,
        )

    pairs = [(0, t) for t in range(1, n_tm)]
    pairs += [(k, t) for t in range(n_tm - 1, -1, -1) for k in range(reach, 0, -1)]
    for k, turn in pairs:

        @pl.when(me >= k)
        def _():
            share(k, turn).start()

    own = pl.multiple_of(my_tm * samples, LANES)
    extended[0:channels, pl.ds(own, samples)] = white[...]
    if len(out_refs) > 1:
        traces, plane = out_refs
        lay_rows(white[...], traces, own, my_tm, n_tm)
    for step in range(1, n_chan):
        spread(step).wait_send()
    tiles = extended.shape[0] // LANES
    laid = 0
    for k in range(reach + 1):
        for turn in range(n_tm):
            if k == 0 and turn == 0:
                continue

            @pl.when(me + k < n_chan)
            def _():
                share(k, turn).wait_recv()

        if len(out_refs) == 1:
            continue
        if k == 0:
            for turn in range(1, n_tm):
                window = lax.rem(my_tm + n_tm - turn, n_tm)
                lanes = pl.multiple_of(window * samples, LANES)
                lay_rows(extended[0:channels, pl.ds(lanes, samples)], traces, lanes, my_tm, n_tm)
        ready = tiles if k == reach else (k + 1) * channels // LANES
        for tile in range(laid, ready):
            lanes = slice(tile * LANES, (tile + 1) * LANES)
            turned = extended[lanes, :].astype(jnp.float32).T.astype(jnp.bfloat16)
            for w in range(n_tm):
                plane[w, samples - SUB : 2 * samples - SUB, lanes] = turned[
                    w * samples : (w + 1) * samples
                ]
        laid = ready

    for k, turn in pairs:

        @pl.when(me >= k)
        def _():
            share(k, turn).wait_send()

    if len(out_refs) == 1:
        out_refs[0][...] = extended[...]


def lay_rows(own, traces, lanes, my_tm, n_tm):
    channels, samples = own.shape
    positive = my_tm
    scale = 1.0 / math.sqrt(samples * n_tm)
    row = lax.broadcasted_iota(jnp.int32, (SUB, samples), 0)
    at = lax.broadcasted_iota(jnp.int32, (SUB, samples), 1) - row + SUB * (1 - positive)
    weight = jnp.where((at >= 0) & (at < samples), scale, 0.0)
    moved = pltpu.roll(own.astype(jnp.float32), (1 - positive) * (samples - SUB), 1)
    for channel in range(channels):
        trace = jnp.broadcast_to(moved[channel : channel + 1], (SUB, samples))
        rolled = pltpu.roll(trace, 0, 1, stride=1, stride_axis=0)
        traces[channel, :, pl.ds(lanes, samples)] = (rolled * weight).astype(jnp.bfloat16)


def prepare(raw_strain, fir_taps, live_mask, n_chan, n_tm, swept):
    _, all_channels, tract_len = raw_strain.shape
    channels = all_channels // n_chan
    samples = tract_len * n_chan // STRIDE
    members = max(1, LANES // tract_len)
    part = channels // members
    width = members * tract_len
    reach = -(-OFF // channels)
    vmem = pl.BlockSpec(memory_space=pltpu.VMEM)
    hbm = pl.BlockSpec(memory_space=pltpu.HBM)
    landing = channels + OFF
    outs = [(landing, n_tm * samples)]
    if swept:
        landing = -(-landing // LANES) * LANES
        outs = [
            (channels, SUB, n_tm * samples),
            (n_tm, 3 * samples - 2 * SUB, landing),
        ]
    return pl.pallas_call(
        functools.partial(prepare_kernel, n_chan, n_tm, members, len(outs)),
        out_shape=[jax.ShapeDtypeStruct(shape, jnp.bfloat16) for shape in outs],
        in_specs=[hbm, hbm, hbm],
        out_specs=[vmem] * len(outs),
        scratch_shapes=[
            pltpu.VMEM((1, tract_len, all_channels), jnp.bfloat16),
            pltpu.VMEM((1, TAPS), jnp.bfloat16),
            pltpu.VMEM((1, channels), jnp.int32),
            pltpu.VMEM((n_chan, part, width), jnp.bfloat16),
            pltpu.VMEM((n_chan, part, width), jnp.bfloat16),
            pltpu.VMEM((members * samples, n_chan * width), jnp.bfloat16),
            pltpu.VMEM((n_chan * width, members * samples), jnp.bfloat16),
            pltpu.VMEM((channels, samples), jnp.bfloat16),
            pltpu.VMEM((landing, n_tm * samples), jnp.bfloat16),
            pltpu.SemaphoreType.DMA((n_chan,)),
            pltpu.SemaphoreType.DMA((n_chan,)),
            pltpu.SemaphoreType.DMA((reach + 1, n_tm)),
            pltpu.SemaphoreType.DMA((reach + 1, n_tm)),
            pltpu.SemaphoreType.DMA((3,)),
        ],
        compiler_params=pltpu.CompilerParams(
            collective_id=0, has_side_effects=True, vmem_limit_bytes=VMEM_GRANT
        ),
        name="prepare",
    )(
        pltpu.with_memory_space_constraint(raw_strain.transpose(0, 2, 1), pltpu.HBM),
        pltpu.with_memory_space_constraint(fir_taps.reshape(1, TAPS), pltpu.HBM),
        pltpu.with_memory_space_constraint(live_mask.reshape(1, channels), pltpu.HBM),
    )


def correlate_kernel(windows, samples, lag_dev, ext_ref, out_ref, wide):
    group = pl.program_id(0)
    first_lag = lax.axis_index("tm") * lag_dev - LAG
    norm_scale = 1.0 / math.sqrt(samples * windows)
    rows = ext_ref.shape[0]

    @pl.when(group == 0)
    def _():
        wide[0:rows, :] = ext_ref[...]
        wide[rows:, :] = jnp.zeros((wide.shape[0] - rows, wide.shape[1]), wide.dtype)

    base = pl.multiple_of(group * SUB, SUB)
    own = wide[pl.ds(base, SUB), :].astype(jnp.float32)
    partners = wide[pl.ds(base, OFF), :]
    beyond = wide[pl.ds(pl.multiple_of(base + OFF, SUB), LANES), :]
    lag = first_lag + lax.broadcasted_iota(jnp.int32, (lag_dev, samples), 0)
    at = lax.broadcasted_iota(jnp.int32, (lag_dev, samples), 1) - lag
    keep = (at >= 0) & (at < samples)
    lane = lax.broadcasted_iota(jnp.int32, (lag_dev, LANES), 1)
    if lag_dev % samples == 0 and LAG % samples == 0:
        turn = None
    else:
        turn = lax.rem(first_lag + samples * (-(-LAG // samples)), samples)
    blocks = []
    for r in range(SUB):
        parts = []
        for w in range(windows):
            trace = own[r : r + 1, w * samples : (w + 1) * samples]
            if turn is not None:
                trace = pltpu.roll(jnp.broadcast_to(trace, (8, samples)), turn, 1)[0:1]
            trace = jnp.broadcast_to(trace, (lag_dev, samples))
            rolled = pltpu.roll(trace, 0, 1, stride=1, stride_axis=0)
            parts.append(jnp.where(keep, rolled, 0.0).astype(jnp.bfloat16))
        blocks.append(jnp.concatenate(parts, axis=1))
    toeplitz = jnp.concatenate(blocks, axis=0)
    contract = (((1,), (1,)), ((), ()))
    near = lax.dot_general(toeplitz, partners, contract, preferred_element_type=jnp.float32)
    far = lax.dot_general(toeplitz, beyond, contract, preferred_element_type=jnp.float32)
    for r in range(SUB):
        first = r * lag_dev
        skip = r + 1
        columns = [
            near[first : first + lag_dev, k * LANES : (k + 1) * LANES] for k in range(OFF // LANES)
        ]
        columns[0] = jnp.where(lane < skip, far[first : first + lag_dev], columns[0])
        columns = [(c * norm_scale).astype(jnp.bfloat16).astype(jnp.float32) for c in columns]
        turned = [pltpu.roll(column, LANES - skip, 1) for column in columns]
        for k in range(len(columns)):
            following = turned[(k + 1) % len(columns)]
            value = jnp.where(lane < LANES - skip, turned[k], following)
            out_ref[r, :, k * LANES : (k + 1) * LANES] = value.astype(jnp.bfloat16)


def correlate(extended, channels, windows, lag_dev):
    depth = extended.shape[1]
    samples = depth // windows
    return pl.pallas_call(
        functools.partial(correlate_kernel, windows, samples, lag_dev),
        out_shape=jax.ShapeDtypeStruct((channels, lag_dev, OFF), jnp.bfloat16),
        grid=(channels // SUB,),
        in_specs=[pl.BlockSpec(extended.shape, lambda g: (0, 0))],
        out_specs=pl.BlockSpec((SUB, lag_dev, OFF), lambda g: (g, 0, 0)),
        scratch_shapes=[pltpu.VMEM((channels - SUB + OFF + LANES, depth), jnp.bfloat16)],
        compiler_params=pltpu.CompilerParams(vmem_limit_bytes=VMEM_GRANT),
        name="correlate",
    )(extended)


def sweep_kernel(windows, samples, traces, plane, out_ref, staged, ship_sem):
    positive = lax.axis_index("tm")
    channels, lag_dev, _ = staged.shape
    pad = samples - SUB
    lane = lax.broadcasted_iota(jnp.int32, (SUB, LANES), 1)
    half = SUB // 2
    groups = channels // (2 * SUB)
    steps = lag_dev // (2 * SUB) * groups

    def place(turn):
        step, odd = divmod(turn, 2)
        return (2 * (step % groups) + odd) * SUB, 2 * (step // groups)

    def weights(turn, band, first_lane, count):
        channel, low = place(turn)
        start = pl.multiple_of((low + band) * SUB + positive * pad, SUB)
        lanes = channel // LANES * LANES + first_lane
        return jnp.concatenate(
            [plane[w, pl.ds(start, samples), lanes : lanes + count] for w in range(windows)], axis=0
        )

    def finish(turn, accs, i):
        channel, low = place(turn)
        part, k = divmod(i, half)
        near = [pltpu.matmul_pop(accs[turn % 2][unit][part][k]) for unit in range(2)]
        far = pltpu.matmul_pop(accs[turn % 2][part][2][k])
        skip = (channel + i) % LANES + 1
        for band in range(2):
            columns = [
                near[band][:, :LANES],
                near[band][:, LANES:],
                far[:, band * LANES : (band + 1) * LANES],
            ]
            values = [
                pltpu.roll(jnp.where(lane < skip, columns[k + 1], columns[k]), LANES - skip, 1)
                for k in range(2)
            ]
            first = (low + band) * SUB
            staged[channel + i, first : first + SUB, :] = jnp.concatenate(values, axis=1).astype(
                jnp.bfloat16
            )

    def launch(turn, accs):
        channel, _ = place(turn)
        odd = turn % 2
        if not odd:
            for unit in range(2):
                pltpu.matmul_push_rhs(weights(turn, unit, 0, OFF), 0, unit)
        count = done = 0
        for kind in (2, 0, 1) if odd else (0, 1, 2):
            for i in range(half):
                staged_rhs = None
                if i == 0 and kind == 0:
                    staged_rhs = 0
                elif i == 0 and kind == 2 and not odd:
                    staged_rhs = 1
                for unit in range(2):
                    part = unit if kind == 2 else kind
                    pltpu.matmul_acc_lhs(
                        accs[odd][unit][kind][i],
                        traces[channel + part * half + i],
                        load_staged_rhs=staged_rhs,
                    )
                if i == 0 and kind == 0 and not odd:
                    for unit in range(2):
                        far = [weights(turn, band, OFF, LANES) for band in range(2)]
                        pltpu.matmul_push_rhs(jnp.concatenate(far, axis=1), 1, unit)
                if i == 0 and kind == 2 and odd:
                    for unit in range(2):
                        pltpu.matmul_push_rhs(weights(turn, unit, 0, OFF), 0, unit)
                count += 1
                while turn and done < SUB * count // (3 * half):
                    finish(turn - 1, accs, done)
                    done += 1

    def ship(turn):
        channel, low = place(turn)
        where = (pl.ds(channel, SUB), pl.ds(low * SUB, 2 * SUB), slice(None))
        return pltpu.make_async_copy(staged.at[where], out_ref.at[where], ship_sem.at[turn])

    def run(*flat):
        flat = iter(flat)
        accs = [[[None] * 3 for _ in range(2)] for _ in range(2)]
        for odd in range(2):
            for unit in range(2):
                for kind in range(3):
                    accs[odd][unit][kind] = [next(flat) for _ in range(half)]
        for turn in range(2 * steps):
            launch(turn, accs)
            if turn:
                ship(turn - 1).start()
        for i in range(SUB):
            finish(2 * steps - 1, accs, i)
        ship(2 * steps - 1).start()

    pl.run_scoped(
        run,
        *[
            pltpu.ACC(unit)((SUB, OFF), jnp.float32)
            for odd in range(2)
            for unit in range(2)
            for _ in range(3 * half)
        ],
    )
    for turn in range(2 * steps):
        ship(turn).wait()


def sweep(traces, plane, lag_dev):
    channels, _, depth = traces.shape
    windows = plane.shape[0]
    turns = lag_dev // (2 * SUB) * (channels // SUB)
    vmem = pl.BlockSpec(memory_space=pltpu.VMEM)
    return pl.pallas_call(
        functools.partial(sweep_kernel, windows, depth // windows),
        out_shape=jax.ShapeDtypeStruct((channels, lag_dev, OFF), jnp.bfloat16),
        in_specs=[vmem, vmem],
        out_specs=pl.BlockSpec(memory_space=pltpu.HBM),
        scratch_shapes=[
            pltpu.VMEM((channels, lag_dev, OFF), jnp.bfloat16),
            pltpu.SemaphoreType.DMA((turns,)),
        ],
        compiler_params=pltpu.CompilerParams(vmem_limit_bytes=VMEM_GRANT),
        name="sweep",
    )(traces, plane)


def shards(raw_strain, fir_taps, live_mask):
    n_chan = lax.axis_size("chan")
    n_tm = lax.axis_size("tm")
    channels = live_mask.shape[0]
    lag_dev = 2 * LAG // n_tm
    samples = raw_strain.shape[2] * n_chan // STRIDE
    swept = n_tm == 2 and samples == LAG == LANES and 2 * samples == OFF
    swept = swept and channels % (2 * SUB) == 0 and channels <= STAGED_CHANNELS
    prepared = prepare(raw_strain, fir_taps, live_mask, n_chan, n_tm, swept)
    if swept:
        return sweep(*prepared, lag_dev)
    return correlate(*prepared, channels, n_tm, lag_dev)


def solution(mesh):
    placed = (P("tm", "fibre", "chan"), P(), P(("fibre", "chan")))
    return jax.shard_map(
        shards,
        mesh=mesh,
        in_specs=placed,
        out_specs=P(("fibre", "chan"), "tm", None),
        check_vma=False,
    )
```

```python
import functools
import math

import jax
import jax.numpy as jnp
from jax import lax
from jax.experimental import pallas as pl
from jax.experimental.pallas import tpu as pltpu
from jax.sharding import PartitionSpec as P

OFF = 256
LAG = 128
TAPS = 64
STRIDE = 4
HIST = 60
LANES = 128
SUB = 16
STAGED_CHANNELS = 256
VMEM_GRANT = 28 * 2**20
MESH = pl.DeviceIdType.MESH


def tap_block(taps_row, member, members, tract_len, rows):
    width = members * tract_len
    tap = lax.broadcasted_iota(jnp.int32, (TAPS, width), 0)
    lane = lax.broadcasted_iota(jnp.int32, (TAPS, width), 1)
    flip = jnp.where(tap + lane == TAPS - 1, 1.0, 0.0).astype(jnp.bfloat16)
    reversed_row = jnp.dot(
        jnp.broadcast_to(taps_row, (8, TAPS)), flip, preferred_element_type=jnp.float32
    )[0:1]
    start = (member * tract_len - HIST) % width
    rolled = pltpu.roll(
        jnp.broadcast_to(reversed_row, (rows, width)), start, 1, stride=STRIDE, stride_axis=0
    )
    row = lax.broadcasted_iota(jnp.int32, (rows, width), 0)
    local = lax.broadcasted_iota(jnp.int32, (rows, width), 1) - member * tract_len
    index = STRIDE * row + STRIDE - 1 - local
    keep = (local >= 0) & (local < tract_len) & (index >= 0) & (index < TAPS)
    return jnp.where(keep, rolled, 0.0).astype(jnp.bfloat16)


def prepare_kernel(
    n_chan,
    n_tm,
    members,
    outs,
    raw_hbm,
    taps_hbm,
    mask_hbm,
    *refs,
):
    out_refs, refs = refs[:outs], refs[outs:]
    (
        raw_ref,
        taps_ref,
        mask_ref,
        packed,
        received,
        fir,
        fir_turned,
        white,
        extended,
        send_a,
        recv_a,
        send_b,
        recv_b,
        load,
    ) = refs
    loads = [
        pltpu.make_async_copy(source, target, load.at[i])
        for i, (source, target) in enumerate(
            [(raw_hbm, raw_ref), (taps_hbm, taps_ref), (mask_hbm, mask_ref)]
        )
    ]
    loads[0].start()
    me = lax.axis_index("chan")
    my_tm = lax.axis_index("tm")
    tract_len = raw_hbm.shape[1]
    channels, samples = white.shape
    part = channels // members
    width = members * tract_len
    outputs = tract_len // STRIDE
    reach = -(-OFF // channels)

    def signal(chan, turn):
        pl.semaphore_signal(
            barrier,
            inc=1,
            device_id={"chan": chan, "tm": lax.rem(my_tm + turn, n_tm)},
            device_id_type=MESH,
        )

    barrier = pltpu.get_barrier_semaphore()
    for step in range(1, n_chan):
        signal(lax.rem(me + step, n_chan), 0)
    for turn in range(1, n_tm):
        signal(me, turn)
        for k in range(1, reach + 1):

            @pl.when(me >= k)
            def _():
                signal(me - k, turn)

            @pl.when(me + k < n_chan)
            def _():
                signal(me + k, turn)

    loads[1].start()
    loads[2].start()
    loads[0].wait()
    turned = raw_ref[0].astype(jnp.float32).T.astype(jnp.bfloat16)
    for block in range(n_chan):
        first = block * channels
        pieces = [turned[first + m * part : first + (m + 1) * part] for m in range(members)]
        packed[block] = jnp.concatenate(pieces, axis=1)
    near_blocks = 1
    for k in range(1, reach + 1):
        near_blocks = near_blocks + (me + n_chan - k) // n_chan + 1 - (me + k) // n_chan
    pl.semaphore_wait(barrier, n_chan - 1 + (n_tm - 1) * near_blocks)

    def spread(target, slot):
        return pltpu.make_async_remote_copy(
            src_ref=packed.at[target],
            dst_ref=received.at[me],
            send_sem=send_a.at[slot],
            recv_sem=recv_a.at[me],
            device_id={"chan": target},
            device_id_type=MESH,
        )

    ways = [(distance, side) for distance in range(n_chan - 1, 0, -1) for side in range(2)]
    for distance, side in ways:
        target = me + distance if side else me - distance

        @pl.when(target < n_chan if side else target >= 0)
        def _():
            spread(target, 2 * distance + side).start()

    received[me] = packed[me]
    loads[1].wait()
    loads[2].wait()
    fir[...] = jnp.zeros_like(fir)
    taps_row = taps_ref[...]
    rows = 2 * outputs
    for m in range(members):
        block = tap_block(taps_row, m, members, tract_len, rows)
        for source in range(n_chan):
            first = m * samples + source * outputs
            count = min(rows, samples - source * outputs)
            fir[first : first + count, source * width : (source + 1) * width] = block[:count]
    fir_turned[...] = fir[...].astype(jnp.float32).T.astype(jnp.bfloat16)
    alive = mask_ref[...].astype(jnp.float32)
    diagonal = lax.broadcasted_iota(jnp.int32, (channels, channels), 0) == lax.broadcasted_iota(
        jnp.int32, (channels, channels), 1
    )
    alive_column = jnp.sum(
        jnp.where(diagonal, jnp.broadcast_to(alive, (channels, channels)), 0.0),
        axis=1,
        keepdims=True,
    )

    for k in range(1, reach + 1):
        count = min(channels, OFF - (k - 1) * channels)

        @pl.when(me + k >= n_chan)
        def _():
            extended[k * channels : k * channels + count, :] = jnp.zeros(
                (count, extended.shape[1]), extended.dtype
            )

    if len(out_refs) > 1:
        traces, plane = out_refs
        plane[...] = jnp.zeros_like(plane)
        tail = extended.shape[0] - channels - OFF
        if tail:
            extended[channels + OFF :, :] = jnp.zeros((tail, extended.shape[1]), extended.dtype)

    for source in range(n_chan):

        @pl.when(me != source)
        def _():
            pltpu.make_async_remote_copy(
                src_ref=packed.at[source],
                dst_ref=received.at[source],
                send_sem=send_a.at[0],
                recv_sem=recv_a.at[source],
                device_id={"chan": source},
                device_id_type=MESH,
            ).wait_recv()

    tracts = jnp.concatenate([received[d] for d in range(n_chan)], axis=1)
    filtered = jnp.dot(tracts, fir_turned[...], preferred_element_type=jnp.float32)
    for m in range(members):
        decimated = filtered[:, m * samples : (m + 1) * samples]
        decimated = decimated.astype(jnp.bfloat16).astype(jnp.float32)
        loudness = jnp.sqrt(jnp.mean(decimated * decimated, axis=1, keepdims=True) + 1e-06)
        gain = alive_column[m * part : (m + 1) * part] / loudness
        white[m * part : (m + 1) * part, :] = (decimated * gain).astype(jnp.bfloat16)

    def share(k, turn):
        count = channels if k == 0 else min(channels, OFF - (k - 1) * channels)
        window = pl.multiple_of(my_tm * samples, LANES)
        return pltpu.make_async_remote_copy(
            src_ref=white.at[pl.ds(0, count), :],
            dst_ref=extended.at[pl.ds(k * channels, count), pl.ds(window, samples)],
            send_sem=send_b.at[k, turn],
            recv_sem=recv_b.at[k, turn],
            device_id={"chan": me - k, "tm": lax.rem(my_tm + turn, n_tm)},
            device_id_type=MESH,
        )

    pairs = [(0, t) for t in range(1, n_tm)]
    pairs += [(k, t) for k in range(reach, 0, -1) for t in range(n_tm - 1, -1, -1)]
    for k, turn in pairs:

        @pl.when(me >= k)
        def _():
            share(k, turn).start()

    own = pl.multiple_of(my_tm * samples, LANES)
    extended[0:channels, pl.ds(own, samples)] = white[...]
    if len(out_refs) > 1:
        traces, plane = out_refs
        lay_rows(white[...], traces, own, my_tm, n_tm)
    for distance, side in ways:
        target = me + distance if side else me - distance

        @pl.when(target < n_chan if side else target >= 0)
        def _():
            spread(target, 2 * distance + side).wait_send()

    tiles = extended.shape[0] // LANES
    offset = pl.multiple_of((1 - my_tm) * (samples - SUB), SUB)
    laid = 0
    for k in range(reach + 1):
        for turn in range(n_tm):
            if k == 0 and turn == 0:
                continue

            @pl.when(me + k < n_chan)
            def _():
                share(k, turn).wait_recv()

        if len(out_refs) == 1:
            continue
        if k == 0:
            for turn in range(1, n_tm):
                window = lax.rem(my_tm + n_tm - turn, n_tm)
                lanes = pl.multiple_of(window * samples, LANES)
                lay_rows(extended[0:channels, pl.ds(lanes, samples)], traces, lanes, my_tm, n_tm)
        ready = tiles if k == reach else (k + 1) * channels // LANES
        for tile in range(laid, ready):
            lanes = slice(tile * LANES, (tile + 1) * LANES)
            turned = extended[lanes, :].astype(jnp.float32).T.astype(jnp.bfloat16)
            for w in range(n_tm):
                plane[w, pl.ds(offset, samples), lanes] = turned[w * samples : (w + 1) * samples]
        laid = ready

    for k, turn in pairs:

        @pl.when(me >= k)
        def _():
            share(k, turn).wait_send()

    if len(out_refs) == 1:
        out_refs[0][...] = extended[...]


def lay_rows(own, traces, lanes, my_tm, n_tm):
    channels, samples = own.shape
    positive = my_tm
    scale = 1.0 / math.sqrt(samples * n_tm)
    row = lax.broadcasted_iota(jnp.int32, (SUB, samples), 0)
    at = lax.broadcasted_iota(jnp.int32, (SUB, samples), 1) - row + SUB * (1 - positive)
    weight = jnp.where((at >= 0) & (at < samples), scale, 0.0)
    moved = pltpu.roll(own.astype(jnp.float32), (1 - positive) * (samples - SUB), 1)
    for channel in range(channels):
        trace = jnp.broadcast_to(moved[channel : channel + 1], (SUB, samples))
        rolled = pltpu.roll(trace, 0, 1, stride=1, stride_axis=0)
        traces[channel, :, pl.ds(lanes, samples)] = (rolled * weight).astype(jnp.bfloat16)


def prepare(raw_strain, fir_taps, live_mask, n_chan, n_tm, swept):
    _, all_channels, tract_len = raw_strain.shape
    channels = all_channels // n_chan
    samples = tract_len * n_chan // STRIDE
    members = max(1, LANES // tract_len)
    part = channels // members
    width = members * tract_len
    reach = -(-OFF // channels)
    vmem = pl.BlockSpec(memory_space=pltpu.VMEM)
    hbm = pl.BlockSpec(memory_space=pltpu.HBM)
    landing = channels + OFF
    outs = [(landing, n_tm * samples)]
    if swept:
        landing = -(-landing // LANES) * LANES
        outs = [
            (channels, SUB, n_tm * samples),
            (n_tm, 2 * samples - SUB, landing),
        ]
    return pl.pallas_call(
        functools.partial(prepare_kernel, n_chan, n_tm, members, len(outs)),
        out_shape=[jax.ShapeDtypeStruct(shape, jnp.bfloat16) for shape in outs],
        in_specs=[hbm, hbm, hbm],
        out_specs=[vmem] * len(outs),
        scratch_shapes=[
            pltpu.VMEM((1, tract_len, all_channels), jnp.bfloat16),
            pltpu.VMEM((1, TAPS), jnp.bfloat16),
            pltpu.VMEM((1, channels), jnp.int32),
            pltpu.VMEM((n_chan, part, width), jnp.bfloat16),
            pltpu.VMEM((n_chan, part, width), jnp.bfloat16),
            pltpu.VMEM((members * samples, n_chan * width), jnp.bfloat16),
            pltpu.VMEM((n_chan * width, members * samples), jnp.bfloat16),
            pltpu.VMEM((channels, samples), jnp.bfloat16),
            pltpu.VMEM((landing, n_tm * samples), jnp.bfloat16),
            pltpu.SemaphoreType.DMA((2 * n_chan,)),
            pltpu.SemaphoreType.DMA((n_chan,)),
            pltpu.SemaphoreType.DMA((reach + 1, n_tm)),
            pltpu.SemaphoreType.DMA((reach + 1, n_tm)),
            pltpu.SemaphoreType.DMA((3,)),
        ],
        compiler_params=pltpu.CompilerParams(
            collective_id=0, has_side_effects=True, vmem_limit_bytes=VMEM_GRANT
        ),
        name="prepare",
    )(
        pltpu.with_memory_space_constraint(raw_strain.transpose(0, 2, 1), pltpu.HBM),
        pltpu.with_memory_space_constraint(fir_taps.reshape(1, TAPS), pltpu.HBM),
        pltpu.with_memory_space_constraint(live_mask.reshape(1, channels), pltpu.HBM),
    )


def correlate_kernel(windows, samples, lag_dev, ext_ref, out_ref, wide):
    group = pl.program_id(0)
    first_lag = lax.axis_index("tm") * lag_dev - LAG
    norm_scale = 1.0 / math.sqrt(samples * windows)
    rows = ext_ref.shape[0]

    @pl.when(group == 0)
    def _():
        wide[0:rows, :] = ext_ref[...]
        wide[rows:, :] = jnp.zeros((wide.shape[0] - rows, wide.shape[1]), wide.dtype)

    base = pl.multiple_of(group * SUB, SUB)
    own = wide[pl.ds(base, SUB), :].astype(jnp.float32)
    partners = wide[pl.ds(base, OFF), :]
    beyond = wide[pl.ds(pl.multiple_of(base + OFF, SUB), LANES), :]
    lag = first_lag + lax.broadcasted_iota(jnp.int32, (lag_dev, samples), 0)
    at = lax.broadcasted_iota(jnp.int32, (lag_dev, samples), 1) - lag
    keep = (at >= 0) & (at < samples)
    lane = lax.broadcasted_iota(jnp.int32, (lag_dev, LANES), 1)
    if lag_dev % samples == 0 and LAG % samples == 0:
        turn = None
    else:
        turn = lax.rem(first_lag + samples * (-(-LAG // samples)), samples)
    blocks = []
    for r in range(SUB):
        parts = []
        for w in range(windows):
            trace = own[r : r + 1, w * samples : (w + 1) * samples]
            if turn is not None:
                trace = pltpu.roll(jnp.broadcast_to(trace, (8, samples)), turn, 1)[0:1]
            trace = jnp.broadcast_to(trace, (lag_dev, samples))
            rolled = pltpu.roll(trace, 0, 1, stride=1, stride_axis=0)
            parts.append(jnp.where(keep, rolled, 0.0).astype(jnp.bfloat16))
        blocks.append(jnp.concatenate(parts, axis=1))
    toeplitz = jnp.concatenate(blocks, axis=0)
    contract = (((1,), (1,)), ((), ()))
    near = lax.dot_general(toeplitz, partners, contract, preferred_element_type=jnp.float32)
    far = lax.dot_general(toeplitz, beyond, contract, preferred_element_type=jnp.float32)
    for r in range(SUB):
        first = r * lag_dev
        skip = r + 1
        columns = [
            near[first : first + lag_dev, k * LANES : (k + 1) * LANES] for k in range(OFF // LANES)
        ]
        columns[0] = jnp.where(lane < skip, far[first : first + lag_dev], columns[0])
        columns = [(c * norm_scale).astype(jnp.bfloat16).astype(jnp.float32) for c in columns]
        turned = [pltpu.roll(column, LANES - skip, 1) for column in columns]
        for k in range(len(columns)):
            following = turned[(k + 1) % len(columns)]
            value = jnp.where(lane < LANES - skip, turned[k], following)
            out_ref[r, :, k * LANES : (k + 1) * LANES] = value.astype(jnp.bfloat16)


def correlate(extended, channels, windows, lag_dev):
    depth = extended.shape[1]
    samples = depth // windows
    return pl.pallas_call(
        functools.partial(correlate_kernel, windows, samples, lag_dev),
        out_shape=jax.ShapeDtypeStruct((channels, lag_dev, OFF), jnp.bfloat16),
        grid=(channels // SUB,),
        in_specs=[pl.BlockSpec(extended.shape, lambda g: (0, 0))],
        out_specs=pl.BlockSpec((SUB, lag_dev, OFF), lambda g: (g, 0, 0)),
        scratch_shapes=[pltpu.VMEM((channels - SUB + OFF + LANES, depth), jnp.bfloat16)],
        compiler_params=pltpu.CompilerParams(vmem_limit_bytes=VMEM_GRANT),
        name="correlate",
    )(extended)


def sweep_kernel(windows, samples, traces, plane, out_ref, staged, ship_sem):
    channels, lag_dev, _ = staged.shape
    lane = lax.broadcasted_iota(jnp.int32, (SUB, LANES), 1)
    half = SUB // 2
    groups = channels // (2 * SUB)
    steps = lag_dev // (2 * SUB) * groups

    def place(turn):
        step, odd = divmod(turn, 2)
        return (2 * (step % groups) + odd) * SUB, 2 * (step // groups)

    def held(turn):
        channel, low = place(turn)
        return channel // LANES, low

    def weights(turn, band, first_lane, count):
        channel, low = place(turn)
        start = (low + band) * SUB
        lanes = channel // LANES * LANES + first_lane
        return jnp.concatenate(
            [plane[w, start : start + samples, lanes : lanes + count] for w in range(windows)], axis=0
        )

    def finish(turn, accs, i):
        channel, low = place(turn)
        part, k = divmod(i, half)
        near = [pltpu.matmul_pop(accs[turn % 2][unit][part][k]) for unit in range(2)]
        far = pltpu.matmul_pop(accs[turn % 2][part][2][k])
        skip = (channel + i) % LANES + 1
        for band in range(2):
            columns = [
                near[band][:, :LANES],
                near[band][:, LANES:],
                far[:, band * LANES : (band + 1) * LANES],
            ]
            values = [
                pltpu.roll(jnp.where(lane < skip, columns[k + 1], columns[k]), LANES - skip, 1)
                for k in range(2)
            ]
            first = (low + band) * SUB
            staged[channel + i, first : first + SUB, :] = jnp.concatenate(values, axis=1).astype(
                jnp.bfloat16
            )

    def launch(turn, accs):
        channel, _ = place(turn)
        odd = turn % 2
        kept = turn and held(turn) == held(turn - 1)
        if not odd and not kept:
            for unit in range(2):
                pltpu.matmul_push_rhs(weights(turn, unit, 0, OFF), 0, unit)
        count = done = 0
        for kind in (2, 0, 1) if odd else (0, 1, 2):
            for i in range(half):
                staged_rhs = None
                if i == 0 and kind == 0 and (odd or not kept):
                    staged_rhs = 0
                elif i == 0 and kind == 2 and not odd:
                    staged_rhs = 1
                for unit in range(2):
                    part = unit if kind == 2 else kind
                    pltpu.matmul_acc_lhs(
                        accs[odd][unit][kind][i],
                        traces[channel + part * half + i],
                        load_staged_rhs=staged_rhs,
                    )
                if i == 0 and kind == 0 and not odd:
                    for unit in range(2):
                        far = [weights(turn, band, OFF, LANES) for band in range(2)]
                        pltpu.matmul_push_rhs(jnp.concatenate(far, axis=1), 1, unit)
                if i == 0 and kind == 2 and odd:
                    for unit in range(2):
                        pltpu.matmul_push_rhs(weights(turn, unit, 0, OFF), 0, unit)
                count += 1
                while turn and done < SUB * count // (3 * half):
                    finish(turn - 1, accs, done)
                    done += 1

    def ship(turn):
        channel, low = place(turn)
        where = (pl.ds(channel, SUB), pl.ds(low * SUB, 2 * SUB), slice(None))
        return pltpu.make_async_copy(staged.at[where], out_ref.at[where], ship_sem.at[turn])

    def run(*flat):
        flat = iter(flat)
        accs = [[[None] * 3 for _ in range(2)] for _ in range(2)]
        for odd in range(2):
            for unit in range(2):
                for kind in range(3):
                    accs[odd][unit][kind] = [next(flat) for _ in range(half)]
        for turn in range(2 * steps):
            launch(turn, accs)
            if turn:
                ship(turn - 1).start()
        for i in range(SUB):
            finish(2 * steps - 1, accs, i)
        ship(2 * steps - 1).start()

    pl.run_scoped(
        run,
        *[
            pltpu.ACC(unit)((SUB, OFF), jnp.float32)
            for odd in range(2)
            for unit in range(2)
            for _ in range(3 * half)
        ],
    )
    for turn in range(2 * steps):
        ship(turn).wait()


def sweep(traces, plane, lag_dev):
    channels, _, depth = traces.shape
    windows = plane.shape[0]
    turns = lag_dev // (2 * SUB) * (channels // SUB)
    vmem = pl.BlockSpec(memory_space=pltpu.VMEM)
    return pl.pallas_call(
        functools.partial(sweep_kernel, windows, depth // windows),
        out_shape=jax.ShapeDtypeStruct((channels, lag_dev, OFF), jnp.bfloat16),
        in_specs=[vmem, vmem],
        out_specs=pl.BlockSpec(memory_space=pltpu.HBM),
        scratch_shapes=[
            pltpu.VMEM((channels, lag_dev, OFF), jnp.bfloat16),
            pltpu.SemaphoreType.DMA((turns,)),
        ],
        compiler_params=pltpu.CompilerParams(vmem_limit_bytes=VMEM_GRANT),
        name="sweep",
    )(traces, plane)


def shards(raw_strain, fir_taps, live_mask):
    n_chan = lax.axis_size("chan")
    n_tm = lax.axis_size("tm")
    channels = live_mask.shape[0]
    lag_dev = 2 * LAG // n_tm
    samples = raw_strain.shape[2] * n_chan // STRIDE
    swept = n_tm == 2 and samples == LAG == LANES and 2 * samples == OFF
    swept = swept and channels % (2 * SUB) == 0 and channels <= STAGED_CHANNELS
    prepared = prepare(raw_strain, fir_taps, live_mask, n_chan, n_tm, swept)
    if swept:
        return sweep(*prepared, lag_dev)
    return correlate(*prepared, channels, n_tm, lag_dev)


def solution(mesh):
    placed = (P("tm", "fibre", "chan"), P(), P(("fibre", "chan")))
    return jax.shard_map(
        shards,
        mesh=mesh,
        in_specs=placed,
        out_specs=P(("fibre", "chan"), "tm", None),
        check_vma=False,
    )
```

```python
import functools
import math

import jax
import jax.numpy as jnp
from jax import lax
from jax.experimental import pallas as pl
from jax.experimental.pallas import tpu as pltpu
from jax.sharding import PartitionSpec as P

OFF = 256
LAG = 128
TAPS = 64
STRIDE = 4
HIST = 60
LANES = 128
SUB = 16
STAGED_CHANNELS = 256
VMEM_GRANT = 28 * 2**20
MESH = pl.DeviceIdType.MESH


def tap_block(taps_row, member, members, tract_len, rows):
    width = members * tract_len
    tap = lax.broadcasted_iota(jnp.int32, (TAPS, width), 0)
    lane = lax.broadcasted_iota(jnp.int32, (TAPS, width), 1)
    flip = jnp.where(tap + lane == TAPS - 1, 1.0, 0.0).astype(jnp.bfloat16)
    reversed_row = jnp.dot(
        jnp.broadcast_to(taps_row, (8, TAPS)), flip, preferred_element_type=jnp.float32
    )[0:1]
    start = (member * tract_len - HIST) % width
    rolled = pltpu.roll(
        jnp.broadcast_to(reversed_row, (rows, width)), start, 1, stride=STRIDE, stride_axis=0
    )
    row = lax.broadcasted_iota(jnp.int32, (rows, width), 0)
    local = lax.broadcasted_iota(jnp.int32, (rows, width), 1) - member * tract_len
    index = STRIDE * row + STRIDE - 1 - local
    keep = (local >= 0) & (local < tract_len) & (index >= 0) & (index < TAPS)
    return jnp.where(keep, rolled, 0.0).astype(jnp.bfloat16)


def prepare_kernel(
    n_chan,
    n_tm,
    members,
    outs,
    raw_hbm,
    taps_hbm,
    mask_hbm,
    *refs,
):
    out_refs, refs = refs[:outs], refs[outs:]
    (
        raw_ref,
        taps_ref,
        mask_ref,
        packed,
        received,
        fir,
        fir_turned,
        white,
        extended,
        send_a,
        recv_a,
        send_b,
        recv_b,
        load,
    ) = refs
    loads = [
        pltpu.make_async_copy(source, target, load.at[i])
        for i, (source, target) in enumerate(
            [(raw_hbm, raw_ref), (taps_hbm, taps_ref), (mask_hbm, mask_ref)]
        )
    ]
    loads[0].start()
    me = lax.axis_index("chan")
    my_tm = lax.axis_index("tm")
    tract_len = raw_hbm.shape[1]
    channels, samples = white.shape
    part = channels // members
    width = members * tract_len
    outputs = tract_len // STRIDE
    reach = -(-OFF // channels)

    def signal(chan, turn):
        pl.semaphore_signal(
            barrier,
            inc=1,
            device_id={"chan": chan, "tm": lax.rem(my_tm + turn, n_tm)},
            device_id_type=MESH,
        )

    barrier = pltpu.get_barrier_semaphore()
    for step in range(1, n_chan):
        signal(lax.rem(me + step, n_chan), 0)
    for turn in range(1, n_tm):
        signal(me, turn)
        for k in range(1, reach + 1):

            @pl.when(me >= k)
            def _():
                signal(me - k, turn)

            @pl.when(me + k < n_chan)
            def _():
                signal(me + k, turn)

    loads[1].start()
    loads[2].start()
    loads[0].wait()
    turned = raw_ref[0].T
    for block in range(n_chan):
        first = block * channels
        pieces = [turned[first + m * part : first + (m + 1) * part] for m in range(members)]
        packed[block] = jnp.concatenate(pieces, axis=1)
    near_blocks = 1
    for k in range(1, reach + 1):
        near_blocks = near_blocks + (me + n_chan - k) // n_chan + 1 - (me + k) // n_chan
    pl.semaphore_wait(barrier, n_chan - 1 + (n_tm - 1) * near_blocks)

    def spread(target, slot):
        return pltpu.make_async_remote_copy(
            src_ref=packed.at[target],
            dst_ref=received.at[me],
            send_sem=send_a.at[slot],
            recv_sem=recv_a.at[me],
            device_id={"chan": target},
            device_id_type=MESH,
        )

    ways = [(distance, side) for distance in range(n_chan - 1, 0, -1) for side in range(2)]
    for distance, side in ways:
        target = me + distance if side else me - distance

        @pl.when(target < n_chan if side else target >= 0)
        def _():
            spread(target, 2 * distance + side).start()

    received[me] = packed[me]
    loads[1].wait()
    loads[2].wait()
    fir[...] = jnp.zeros_like(fir)
    taps_row = taps_ref[...]
    rows = 2 * outputs
    for m in range(members):
        block = tap_block(taps_row, m, members, tract_len, rows)
        for source in range(n_chan):
            first = m * samples + source * outputs
            count = min(rows, samples - source * outputs)
            fir[first : first + count, source * width : (source + 1) * width] = block[:count]
    fir_turned[...] = fir[...].astype(jnp.float32).T.astype(jnp.bfloat16)
    alive = mask_ref[...].astype(jnp.float32)
    diagonal = lax.broadcasted_iota(jnp.int32, (channels, channels), 0) == lax.broadcasted_iota(
        jnp.int32, (channels, channels), 1
    )
    alive_column = jnp.sum(
        jnp.where(diagonal, jnp.broadcast_to(alive, (channels, channels)), 0.0),
        axis=1,
        keepdims=True,
    )

    for k in range(1, reach + 1):
        count = min(channels, OFF - (k - 1) * channels)

        @pl.when(me + k >= n_chan)
        def _():
            extended[k * channels : k * channels + count, :] = jnp.zeros(
                (count, extended.shape[1]), extended.dtype
            )

    if len(out_refs) > 1:
        traces, plane = out_refs
        plane[...] = jnp.zeros_like(plane)
        tail = extended.shape[0] - channels - OFF
        if tail:
            extended[channels + OFF :, :] = jnp.zeros((tail, extended.shape[1]), extended.dtype)

    for source in range(n_chan):

        @pl.when(me != source)
        def _():
            pltpu.make_async_remote_copy(
                src_ref=packed.at[source],
                dst_ref=received.at[source],
                send_sem=send_a.at[0],
                recv_sem=recv_a.at[source],
                device_id={"chan": source},
                device_id_type=MESH,
            ).wait_recv()

    tracts = jnp.concatenate([received[d] for d in range(n_chan)], axis=1)
    filtered = jnp.dot(tracts, fir_turned[...], preferred_element_type=jnp.float32)
    for m in range(members):
        decimated = filtered[:, m * samples : (m + 1) * samples]
        decimated = decimated.astype(jnp.bfloat16).astype(jnp.float32)
        loudness = jnp.sqrt(jnp.mean(decimated * decimated, axis=1, keepdims=True) + 1e-06)
        gain = alive_column[m * part : (m + 1) * part] / loudness
        white[m * part : (m + 1) * part, :] = (decimated * gain).astype(jnp.bfloat16)

    def share(k, turn):
        count = channels if k == 0 else min(channels, OFF - (k - 1) * channels)
        window = pl.multiple_of(my_tm * samples, LANES)
        return pltpu.make_async_remote_copy(
            src_ref=white.at[pl.ds(0, count), :],
            dst_ref=extended.at[pl.ds(k * channels, count), pl.ds(window, samples)],
            send_sem=send_b.at[k, turn],
            recv_sem=recv_b.at[k, turn],
            device_id={"chan": me - k, "tm": lax.rem(my_tm + turn, n_tm)},
            device_id_type=MESH,
        )

    pairs = [(0, t) for t in range(1, n_tm)]
    pairs += [(k, t) for k in range(reach, 0, -1) for t in range(n_tm - 1, -1, -1)]
    for k, turn in pairs:

        @pl.when(me >= k)
        def _():
            share(k, turn).start()

    own = pl.multiple_of(my_tm * samples, LANES)
    extended[0:channels, pl.ds(own, samples)] = white[...]
    if len(out_refs) > 1:
        traces, plane = out_refs
        lay_rows(white[...], traces, own, my_tm, n_tm)
    for distance, side in ways:
        target = me + distance if side else me - distance

        @pl.when(target < n_chan if side else target >= 0)
        def _():
            spread(target, 2 * distance + side).wait_send()

    tiles = extended.shape[0] // LANES
    offset = pl.multiple_of((1 - my_tm) * (samples - SUB), SUB)
    laid, arrived = set(), set()
    for k in [0, *range(reach, 0, -1)]:
        for turn in range(n_tm):
            if k == 0 and turn == 0:
                continue

            @pl.when(me + k < n_chan)
            def _():
                share(k, turn).wait_recv()

        if len(out_refs) == 1:
            continue
        if k == 0:
            for turn in range(1, n_tm):
                window = lax.rem(my_tm + n_tm - turn, n_tm)
                lanes = pl.multiple_of(window * samples, LANES)
                lay_rows(extended[0:channels, pl.ds(lanes, samples)], traces, lanes, my_tm, n_tm)
        arrived.add(k)
        for tile in range(tiles):
            blocks = {min(row // channels, reach) for row in range(tile * LANES, (tile + 1) * LANES)}
            if tile in laid or not blocks <= arrived:
                continue
            laid.add(tile)
            lanes = slice(tile * LANES, (tile + 1) * LANES)
            turned = extended[lanes, :].astype(jnp.float32).T.astype(jnp.bfloat16)
            for w in range(n_tm):
                plane[w, pl.ds(offset, samples), lanes] = turned[w * samples : (w + 1) * samples]

    for k, turn in pairs:

        @pl.when(me >= k)
        def _():
            share(k, turn).wait_send()

    if len(out_refs) == 1:
        out_refs[0][...] = extended[...]


def lay_rows(own, traces, lanes, my_tm, n_tm):
    channels, samples = own.shape
    positive = my_tm
    scale = 1.0 / math.sqrt(samples * n_tm)
    row = lax.broadcasted_iota(jnp.int32, (SUB, samples), 0)
    at = lax.broadcasted_iota(jnp.int32, (SUB, samples), 1) - row + SUB * (1 - positive)
    weight = jnp.where((at >= 0) & (at < samples), scale, 0.0)
    moved = pltpu.roll(own.astype(jnp.float32), (1 - positive) * (samples - SUB), 1)
    for channel in range(channels):
        trace = jnp.broadcast_to(moved[channel : channel + 1], (SUB, samples))
        rolled = pltpu.roll(trace, 0, 1, stride=1, stride_axis=0)
        traces[channel, :, pl.ds(lanes, samples)] = (rolled * weight).astype(jnp.bfloat16)


def prepare(raw_strain, fir_taps, live_mask, n_chan, n_tm, swept):
    _, all_channels, tract_len = raw_strain.shape
    channels = all_channels // n_chan
    samples = tract_len * n_chan // STRIDE
    members = max(1, LANES // tract_len)
    part = channels // members
    width = members * tract_len
    reach = -(-OFF // channels)
    vmem = pl.BlockSpec(memory_space=pltpu.VMEM)
    hbm = pl.BlockSpec(memory_space=pltpu.HBM)
    landing = channels + OFF
    outs = [(landing, n_tm * samples)]
    if swept:
        landing = -(-landing // LANES) * LANES
        outs = [
            (channels, SUB, n_tm * samples),
            (n_tm, 2 * samples - SUB, landing),
        ]
    return pl.pallas_call(
        functools.partial(prepare_kernel, n_chan, n_tm, members, len(outs)),
        out_shape=[jax.ShapeDtypeStruct(shape, jnp.bfloat16) for shape in outs],
        in_specs=[hbm, hbm, hbm],
        out_specs=[vmem] * len(outs),
        scratch_shapes=[
            pltpu.VMEM((1, tract_len, all_channels), jnp.bfloat16),
            pltpu.VMEM((1, TAPS), jnp.bfloat16),
            pltpu.VMEM((1, channels), jnp.int32),
            pltpu.VMEM((n_chan, part, width), jnp.bfloat16),
            pltpu.VMEM((n_chan, part, width), jnp.bfloat16),
            pltpu.VMEM((members * samples, n_chan * width), jnp.bfloat16),
            pltpu.VMEM((n_chan * width, members * samples), jnp.bfloat16),
            pltpu.VMEM((channels, samples), jnp.bfloat16),
            pltpu.VMEM((landing, n_tm * samples), jnp.bfloat16),
            pltpu.SemaphoreType.DMA((2 * n_chan,)),
            pltpu.SemaphoreType.DMA((n_chan,)),
            pltpu.SemaphoreType.DMA((reach + 1, n_tm)),
            pltpu.SemaphoreType.DMA((reach + 1, n_tm)),
            pltpu.SemaphoreType.DMA((3,)),
        ],
        compiler_params=pltpu.CompilerParams(
            collective_id=0, has_side_effects=True, vmem_limit_bytes=VMEM_GRANT
        ),
        name="prepare",
    )(
        pltpu.with_memory_space_constraint(raw_strain.transpose(0, 2, 1), pltpu.HBM),
        pltpu.with_memory_space_constraint(fir_taps.reshape(1, TAPS), pltpu.HBM),
        pltpu.with_memory_space_constraint(live_mask.reshape(1, channels), pltpu.HBM),
    )


def correlate_kernel(windows, samples, lag_dev, ext_ref, out_ref, wide):
    group = pl.program_id(0)
    first_lag = lax.axis_index("tm") * lag_dev - LAG
    norm_scale = 1.0 / math.sqrt(samples * windows)
    rows = ext_ref.shape[0]

    @pl.when(group == 0)
    def _():
        wide[0:rows, :] = ext_ref[...]
        wide[rows:, :] = jnp.zeros((wide.shape[0] - rows, wide.shape[1]), wide.dtype)

    base = pl.multiple_of(group * SUB, SUB)
    own = wide[pl.ds(base, SUB), :].astype(jnp.float32)
    partners = wide[pl.ds(base, OFF), :]
    beyond = wide[pl.ds(pl.multiple_of(base + OFF, SUB), LANES), :]
    lag = first_lag + lax.broadcasted_iota(jnp.int32, (lag_dev, samples), 0)
    at = lax.broadcasted_iota(jnp.int32, (lag_dev, samples), 1) - lag
    keep = (at >= 0) & (at < samples)
    lane = lax.broadcasted_iota(jnp.int32, (lag_dev, LANES), 1)
    if lag_dev % samples == 0 and LAG % samples == 0:
        turn = None
    else:
        turn = lax.rem(first_lag + samples * (-(-LAG // samples)), samples)
    blocks = []
    for r in range(SUB):
        parts = []
        for w in range(windows):
            trace = own[r : r + 1, w * samples : (w + 1) * samples]
            if turn is not None:
                trace = pltpu.roll(jnp.broadcast_to(trace, (8, samples)), turn, 1)[0:1]
            trace = jnp.broadcast_to(trace, (lag_dev, samples))
            rolled = pltpu.roll(trace, 0, 1, stride=1, stride_axis=0)
            parts.append(jnp.where(keep, rolled, 0.0).astype(jnp.bfloat16))
        blocks.append(jnp.concatenate(parts, axis=1))
    toeplitz = jnp.concatenate(blocks, axis=0)
    contract = (((1,), (1,)), ((), ()))
    near = lax.dot_general(toeplitz, partners, contract, preferred_element_type=jnp.float32)
    far = lax.dot_general(toeplitz, beyond, contract, preferred_element_type=jnp.float32)
    for r in range(SUB):
        first = r * lag_dev
        skip = r + 1
        columns = [
            near[first : first + lag_dev, k * LANES : (k + 1) * LANES] for k in range(OFF // LANES)
        ]
        columns[0] = jnp.where(lane < skip, far[first : first + lag_dev], columns[0])
        columns = [(c * norm_scale).astype(jnp.bfloat16).astype(jnp.float32) for c in columns]
        turned = [pltpu.roll(column, LANES - skip, 1) for column in columns]
        for k in range(len(columns)):
            following = turned[(k + 1) % len(columns)]
            value = jnp.where(lane < LANES - skip, turned[k], following)
            out_ref[r, :, k * LANES : (k + 1) * LANES] = value.astype(jnp.bfloat16)


def correlate(extended, channels, windows, lag_dev):
    depth = extended.shape[1]
    samples = depth // windows
    return pl.pallas_call(
        functools.partial(correlate_kernel, windows, samples, lag_dev),
        out_shape=jax.ShapeDtypeStruct((channels, lag_dev, OFF), jnp.bfloat16),
        grid=(channels // SUB,),
        in_specs=[pl.BlockSpec(extended.shape, lambda g: (0, 0))],
        out_specs=pl.BlockSpec((SUB, lag_dev, OFF), lambda g: (g, 0, 0)),
        scratch_shapes=[pltpu.VMEM((channels - SUB + OFF + LANES, depth), jnp.bfloat16)],
        compiler_params=pltpu.CompilerParams(vmem_limit_bytes=VMEM_GRANT),
        name="correlate",
    )(extended)


def sweep_kernel(windows, samples, traces, plane, out_ref, staged, ship_sem):
    channels, lag_dev, _ = staged.shape
    lane = lax.broadcasted_iota(jnp.int32, (SUB, LANES), 1)
    half = SUB // 2
    groups = channels // (2 * SUB)
    steps = lag_dev // (2 * SUB) * groups

    def place(turn):
        step, odd = divmod(turn, 2)
        return (2 * (step % groups) + odd) * SUB, 2 * (step // groups)

    def held(turn):
        channel, low = place(turn)
        return channel // LANES, low

    def weights(turn, band, first_lane, count):
        channel, low = place(turn)
        start = (low + band) * SUB
        lanes = channel // LANES * LANES + first_lane
        return jnp.concatenate(
            [plane[w, start : start + samples, lanes : lanes + count] for w in range(windows)], axis=0
        )

    def finish(turn, accs, i):
        channel, low = place(turn)
        part, k = divmod(i, half)
        near = [pltpu.matmul_pop(accs[turn % 2][unit][part][k]) for unit in range(2)]
        far = pltpu.matmul_pop(accs[turn % 2][part][2][k])
        skip = (channel + i) % LANES + 1
        for band in range(2):
            columns = [
                near[band][:, :LANES],
                near[band][:, LANES:],
                far[:, band * LANES : (band + 1) * LANES],
            ]
            values = [
                pltpu.roll(jnp.where(lane < skip, columns[k + 1], columns[k]), LANES - skip, 1)
                for k in range(2)
            ]
            first = (low + band) * SUB
            staged[channel + i, first : first + SUB, :] = jnp.concatenate(values, axis=1).astype(
                jnp.bfloat16
            )

    def launch(turn, accs):
        channel, _ = place(turn)
        odd = turn % 2
        kept = turn and held(turn) == held(turn - 1)
        if not odd and not kept:
            for unit in range(2):
                pltpu.matmul_push_rhs(weights(turn, unit, 0, OFF), 0, unit)
        count = done = 0
        for kind in (2, 0, 1) if odd else (0, 1, 2):
            for i in range(half):
                staged_rhs = None
                if i == 0 and kind == 0 and (odd or not kept):
                    staged_rhs = 0
                elif i == 0 and kind == 2 and not odd:
                    staged_rhs = 1
                for unit in range(2):
                    part = unit if kind == 2 else kind
                    pltpu.matmul_acc_lhs(
                        accs[odd][unit][kind][i],
                        traces[channel + part * half + i],
                        load_staged_rhs=staged_rhs,
                    )
                if i == 0 and kind == 0 and not odd:
                    for unit in range(2):
                        far = [weights(turn, band, OFF, LANES) for band in range(2)]
                        pltpu.matmul_push_rhs(jnp.concatenate(far, axis=1), 1, unit)
                if i == 0 and kind == 2 and odd:
                    for unit in range(2):
                        pltpu.matmul_push_rhs(weights(turn, unit, 0, OFF), 0, unit)
                count += 1
                while turn and done < SUB * count // (3 * half):
                    finish(turn - 1, accs, done)
                    done += 1

    def ship(turn):
        channel, low = place(turn)
        where = (pl.ds(channel, SUB), pl.ds(low * SUB, 2 * SUB), slice(None))
        return pltpu.make_async_copy(staged.at[where], out_ref.at[where], ship_sem.at[turn])

    def run(*flat):
        flat = iter(flat)
        accs = [[[None] * 3 for _ in range(2)] for _ in range(2)]
        for odd in range(2):
            for unit in range(2):
                for kind in range(3):
                    accs[odd][unit][kind] = [next(flat) for _ in range(half)]
        for turn in range(2 * steps):
            launch(turn, accs)
            if turn:
                ship(turn - 1).start()
        for i in range(SUB):
            finish(2 * steps - 1, accs, i)
        ship(2 * steps - 1).start()

    pl.run_scoped(
        run,
        *[
            pltpu.ACC(unit)((SUB, OFF), jnp.float32)
            for odd in range(2)
            for unit in range(2)
            for _ in range(3 * half)
        ],
    )
    for turn in range(2 * steps):
        ship(turn).wait()


def sweep(traces, plane, lag_dev):
    channels, _, depth = traces.shape
    windows = plane.shape[0]
    turns = lag_dev // (2 * SUB) * (channels // SUB)
    vmem = pl.BlockSpec(memory_space=pltpu.VMEM)
    return pl.pallas_call(
        functools.partial(sweep_kernel, windows, depth // windows),
        out_shape=jax.ShapeDtypeStruct((channels, lag_dev, OFF), jnp.bfloat16),
        in_specs=[vmem, vmem],
        out_specs=pl.BlockSpec(memory_space=pltpu.HBM),
        scratch_shapes=[
            pltpu.VMEM((channels, lag_dev, OFF), jnp.bfloat16),
            pltpu.SemaphoreType.DMA((turns,)),
        ],
        compiler_params=pltpu.CompilerParams(vmem_limit_bytes=VMEM_GRANT),
        name="sweep",
    )(traces, plane)


def shards(raw_strain, fir_taps, live_mask):
    n_chan = lax.axis_size("chan")
    n_tm = lax.axis_size("tm")
    channels = live_mask.shape[0]
    lag_dev = 2 * LAG // n_tm
    samples = raw_strain.shape[2] * n_chan // STRIDE
    swept = n_tm == 2 and samples == LAG == LANES and 2 * samples == OFF
    swept = swept and channels % (2 * SUB) == 0 and channels <= STAGED_CHANNELS
    prepared = prepare(raw_strain, fir_taps, live_mask, n_chan, n_tm, swept)
    if swept:
        return sweep(*prepared, lag_dev)
    return correlate(*prepared, channels, n_tm, lag_dev)


def solution(mesh):
    placed = (P("tm", "fibre", "chan"), P(), P(("fibre", "chan")))
    return jax.shard_map(
        shards,
        mesh=mesh,
        in_specs=placed,
        out_specs=P(("fibre", "chan"), "tm", None),
        check_vma=False,
    )
```

```python
import functools
import math

import jax
import jax.numpy as jnp
from jax import lax
from jax.experimental import pallas as pl
from jax.experimental.pallas import tpu as pltpu
from jax.sharding import PartitionSpec as P

OFF = 256
LAG = 128
TAPS = 64
STRIDE = 4
HIST = 60
LANES = 128
SUB = 16
STAGED_CHANNELS = 256
VMEM_GRANT = 28 * 2**20
MESH = pl.DeviceIdType.MESH


def tap_block(taps_row, member, members, tract_len, rows):
    width = members * tract_len
    tap = lax.broadcasted_iota(jnp.int32, (TAPS, width), 0)
    lane = lax.broadcasted_iota(jnp.int32, (TAPS, width), 1)
    flip = jnp.where(tap + lane == TAPS - 1, 1.0, 0.0).astype(jnp.bfloat16)
    reversed_row = jnp.dot(
        jnp.broadcast_to(taps_row, (8, TAPS)), flip, preferred_element_type=jnp.float32
    )[0:1]
    start = (member * tract_len - HIST) % width
    rolled = pltpu.roll(
        jnp.broadcast_to(reversed_row, (rows, width)), start, 1, stride=STRIDE, stride_axis=0
    )
    row = lax.broadcasted_iota(jnp.int32, (rows, width), 0)
    local = lax.broadcasted_iota(jnp.int32, (rows, width), 1) - member * tract_len
    index = STRIDE * row + STRIDE - 1 - local
    keep = (local >= 0) & (local < tract_len) & (index >= 0) & (index < TAPS)
    return jnp.where(keep, rolled, 0.0).astype(jnp.bfloat16)


def prepare_kernel(
    n_chan,
    n_tm,
    members,
    outs,
    raw_hbm,
    taps_hbm,
    mask_hbm,
    *refs,
):
    out_refs, refs = refs[:outs], refs[outs:]
    (
        raw_ref,
        taps_ref,
        mask_ref,
        packed,
        received,
        fir,
        fir_turned,
        white,
        extended,
        send_a,
        recv_a,
        send_b,
        recv_b,
        load,
    ) = refs
    loads = [
        pltpu.make_async_copy(source, target, load.at[i])
        for i, (source, target) in enumerate(
            [(raw_hbm, raw_ref), (taps_hbm, taps_ref), (mask_hbm, mask_ref)]
        )
    ]
    loads[0].start()
    me = lax.axis_index("chan")
    my_tm = lax.axis_index("tm")
    tract_len = raw_hbm.shape[1]
    channels, samples = white.shape
    part = channels // members
    width = members * tract_len
    outputs = tract_len // STRIDE
    reach = -(-OFF // channels)

    def signal(chan, turn):
        pl.semaphore_signal(
            barrier,
            inc=1,
            device_id={"chan": chan, "tm": lax.rem(my_tm + turn, n_tm)},
            device_id_type=MESH,
        )

    barrier = pltpu.get_barrier_semaphore()
    for step in range(1, n_chan):
        signal(lax.rem(me + step, n_chan), 0)
    for turn in range(1, n_tm):
        signal(me, turn)
        for k in range(1, reach + 1):

            @pl.when(me >= k)
            def _():
                signal(me - k, turn)

            @pl.when(me + k < n_chan)
            def _():
                signal(me + k, turn)

    loads[1].start()
    loads[2].start()
    loads[0].wait()
    turned = raw_ref[0].astype(jnp.float32).T.astype(jnp.bfloat16)
    for block in range(n_chan):
        first = block * channels
        pieces = [turned[first + m * part : first + (m + 1) * part] for m in range(members)]
        packed[block] = jnp.concatenate(pieces, axis=1)
    near_blocks = 1
    for k in range(1, reach + 1):
        near_blocks = near_blocks + (me + n_chan - k) // n_chan + 1 - (me + k) // n_chan
    pl.semaphore_wait(barrier, n_chan - 1 + (n_tm - 1) * near_blocks)

    def spread(target, slot):
        return pltpu.make_async_remote_copy(
            src_ref=packed.at[target],
            dst_ref=received.at[me],
            send_sem=send_a.at[slot],
            recv_sem=recv_a.at[me],
            device_id={"chan": target},
            device_id_type=MESH,
        )

    ways = [(distance, side) for distance in range(n_chan - 1, 0, -1) for side in range(2)]
    for distance, side in ways:
        target = me + distance if side else me - distance

        @pl.when(target < n_chan if side else target >= 0)
        def _():
            spread(target, 2 * distance + side).start()

    received[me] = packed[me]
    loads[1].wait()
    loads[2].wait()
    fir[...] = jnp.zeros_like(fir)
    taps_row = taps_ref[...]
    rows = 2 * outputs
    for m in range(members):
        block = tap_block(taps_row, m, members, tract_len, rows)
        for source in range(n_chan):
            first = m * samples + source * outputs
            count = min(rows, samples - source * outputs)
            fir[first : first + count, source * width : (source + 1) * width] = block[:count]
    fir_turned[...] = fir[...].astype(jnp.float32).T.astype(jnp.bfloat16)
    alive = mask_ref[...].astype(jnp.float32)
    diagonal = lax.broadcasted_iota(jnp.int32, (channels, channels), 0) == lax.broadcasted_iota(
        jnp.int32, (channels, channels), 1
    )
    alive_column = jnp.sum(
        jnp.where(diagonal, jnp.broadcast_to(alive, (channels, channels)), 0.0),
        axis=1,
        keepdims=True,
    )

    for k in range(1, reach + 1):
        count = min(channels, OFF - (k - 1) * channels)

        @pl.when(me + k >= n_chan)
        def _():
            extended[k * channels : k * channels + count, :] = jnp.zeros(
                (count, extended.shape[1]), extended.dtype
            )

    if len(out_refs) > 1:
        traces, plane = out_refs
        plane[...] = jnp.zeros_like(plane)
        tail = extended.shape[0] - channels - OFF
        if tail:
            extended[channels + OFF :, :] = jnp.zeros((tail, extended.shape[1]), extended.dtype)

    for source in range(n_chan):

        @pl.when(me != source)
        def _():
            pltpu.make_async_remote_copy(
                src_ref=packed.at[source],
                dst_ref=received.at[source],
                send_sem=send_a.at[0],
                recv_sem=recv_a.at[source],
                device_id={"chan": source},
                device_id_type=MESH,
            ).wait_recv()

    tracts = jnp.concatenate([received[d] for d in range(n_chan)], axis=1)
    filtered = jnp.dot(tracts, fir_turned[...], preferred_element_type=jnp.float32)
    for m in range(members):
        decimated = filtered[:, m * samples : (m + 1) * samples]
        decimated = decimated.astype(jnp.bfloat16).astype(jnp.float32)
        loudness = jnp.sqrt(jnp.mean(decimated * decimated, axis=1, keepdims=True) + 1e-06)
        gain = alive_column[m * part : (m + 1) * part] / loudness
        white[m * part : (m + 1) * part, :] = (decimated * gain).astype(jnp.bfloat16)

    def share(k, turn):
        count = channels if k == 0 else min(channels, OFF - (k - 1) * channels)
        window = pl.multiple_of(my_tm * samples, LANES)
        return pltpu.make_async_remote_copy(
            src_ref=white.at[pl.ds(0, count), :],
            dst_ref=extended.at[pl.ds(k * channels, count), pl.ds(window, samples)],
            send_sem=send_b.at[k, turn],
            recv_sem=recv_b.at[k, turn],
            device_id={"chan": me - k, "tm": lax.rem(my_tm + turn, n_tm)},
            device_id_type=MESH,
        )

    pairs = [(0, t) for t in range(1, n_tm)]
    pairs += [(k, t) for k in range(reach, 0, -1) for t in range(n_tm - 1, -1, -1)]
    for k, turn in pairs:

        @pl.when(me >= k)
        def _():
            share(k, turn).start()

    own = pl.multiple_of(my_tm * samples, LANES)
    extended[0:channels, pl.ds(own, samples)] = white[...]
    if len(out_refs) > 1:
        traces, plane = out_refs
        lay_rows(white[...], traces, own, my_tm, n_tm)
    for distance, side in ways:
        target = me + distance if side else me - distance

        @pl.when(target < n_chan if side else target >= 0)
        def _():
            spread(target, 2 * distance + side).wait_send()

    tiles = extended.shape[0] // LANES
    offset = pl.multiple_of((1 - my_tm) * (samples - SUB), SUB)
    laid = 0
    for k in range(reach + 1):
        for turn in range(n_tm):
            if k == 0 and turn == 0:
                continue

            @pl.when(me + k < n_chan)
            def _():
                share(k, turn).wait_recv()

        if len(out_refs) == 1:
            continue
        if k == 0:
            for turn in range(1, n_tm):
                window = lax.rem(my_tm + n_tm - turn, n_tm)
                lanes = pl.multiple_of(window * samples, LANES)
                lay_rows(extended[0:channels, pl.ds(lanes, samples)], traces, lanes, my_tm, n_tm)
        ready = tiles if k == reach else (k + 1) * channels // LANES
        for tile in range(laid, ready):
            lanes = slice(tile * LANES, (tile + 1) * LANES)
            turned = extended[lanes, :].astype(jnp.float32).T.astype(jnp.bfloat16)
            for w in range(n_tm):
                plane[w, pl.ds(offset, samples), lanes] = turned[w * samples : (w + 1) * samples]
        laid = ready

    for k, turn in pairs:

        @pl.when(me >= k)
        def _():
            share(k, turn).wait_send()

    if len(out_refs) == 1:
        out_refs[0][...] = extended[...]


def lay_rows(own, traces, lanes, my_tm, n_tm):
    channels, samples = own.shape
    positive = my_tm
    scale = 1.0 / math.sqrt(samples * n_tm)
    row = lax.broadcasted_iota(jnp.int32, (SUB, samples), 0)
    at = lax.broadcasted_iota(jnp.int32, (SUB, samples), 1) - row + SUB * (1 - positive)
    weight = jnp.where((at >= 0) & (at < samples), scale, 0.0)
    moved = pltpu.roll(own.astype(jnp.float32), (1 - positive) * (samples - SUB), 1)
    for channel in range(channels):
        trace = jnp.broadcast_to(moved[channel : channel + 1], (SUB, samples))
        rolled = pltpu.roll(trace, 0, 1, stride=1, stride_axis=0)
        traces[channel, :, pl.ds(lanes, samples)] = (rolled * weight).astype(jnp.bfloat16)


def prepare(raw_strain, fir_taps, live_mask, n_chan, n_tm, swept):
    _, all_channels, tract_len = raw_strain.shape
    channels = all_channels // n_chan
    samples = tract_len * n_chan // STRIDE
    members = max(1, LANES // tract_len)
    part = channels // members
    width = members * tract_len
    reach = -(-OFF // channels)
    vmem = pl.BlockSpec(memory_space=pltpu.VMEM)
    hbm = pl.BlockSpec(memory_space=pltpu.HBM)
    landing = channels + OFF
    outs = [(landing, n_tm * samples)]
    if swept:
        landing = -(-landing // LANES) * LANES
        outs = [
            (channels, SUB, n_tm * samples),
            (n_tm, 2 * samples - SUB, landing),
        ]
    return pl.pallas_call(
        functools.partial(prepare_kernel, n_chan, n_tm, members, len(outs)),
        out_shape=[jax.ShapeDtypeStruct(shape, jnp.bfloat16) for shape in outs],
        in_specs=[hbm, hbm, hbm],
        out_specs=[vmem] * len(outs),
        scratch_shapes=[
            pltpu.VMEM((1, tract_len, all_channels), jnp.bfloat16),
            pltpu.VMEM((1, TAPS), jnp.bfloat16),
            pltpu.VMEM((1, channels), jnp.int32),
            pltpu.VMEM((n_chan, part, width), jnp.bfloat16),
            pltpu.VMEM((n_chan, part, width), jnp.bfloat16),
            pltpu.VMEM((members * samples, n_chan * width), jnp.bfloat16),
            pltpu.VMEM((n_chan * width, members * samples), jnp.bfloat16),
            pltpu.VMEM((channels, samples), jnp.bfloat16),
            pltpu.VMEM((landing, n_tm * samples), jnp.bfloat16),
            pltpu.SemaphoreType.DMA((2 * n_chan,)),
            pltpu.SemaphoreType.DMA((n_chan,)),
            pltpu.SemaphoreType.DMA((reach + 1, n_tm)),
            pltpu.SemaphoreType.DMA((reach + 1, n_tm)),
            pltpu.SemaphoreType.DMA((3,)),
        ],
        compiler_params=pltpu.CompilerParams(
            collective_id=0, has_side_effects=True, vmem_limit_bytes=VMEM_GRANT
        ),
        name="prepare",
    )(
        pltpu.with_memory_space_constraint(raw_strain.transpose(0, 2, 1), pltpu.HBM),
        pltpu.with_memory_space_constraint(fir_taps.reshape(1, TAPS), pltpu.HBM),
        pltpu.with_memory_space_constraint(live_mask.reshape(1, channels), pltpu.HBM),
    )


def correlate_kernel(windows, samples, lag_dev, ext_ref, out_ref, wide):
    group = pl.program_id(0)
    first_lag = lax.axis_index("tm") * lag_dev - LAG
    norm_scale = 1.0 / math.sqrt(samples * windows)
    rows = ext_ref.shape[0]

    @pl.when(group == 0)
    def _():
        wide[0:rows, :] = ext_ref[...]
        wide[rows:, :] = jnp.zeros((wide.shape[0] - rows, wide.shape[1]), wide.dtype)

    base = pl.multiple_of(group * SUB, SUB)
    own = wide[pl.ds(base, SUB), :].astype(jnp.float32)
    partners = wide[pl.ds(base, OFF), :]
    beyond = wide[pl.ds(pl.multiple_of(base + OFF, SUB), LANES), :]
    lag = first_lag + lax.broadcasted_iota(jnp.int32, (lag_dev, samples), 0)
    at = lax.broadcasted_iota(jnp.int32, (lag_dev, samples), 1) - lag
    keep = (at >= 0) & (at < samples)
    lane = lax.broadcasted_iota(jnp.int32, (lag_dev, LANES), 1)
    if lag_dev % samples == 0 and LAG % samples == 0:
        turn = None
    else:
        turn = lax.rem(first_lag + samples * (-(-LAG // samples)), samples)
    blocks = []
    for r in range(SUB):
        parts = []
        for w in range(windows):
            trace = own[r : r + 1, w * samples : (w + 1) * samples]
            if turn is not None:
                trace = pltpu.roll(jnp.broadcast_to(trace, (8, samples)), turn, 1)[0:1]
            trace = jnp.broadcast_to(trace, (lag_dev, samples))
            rolled = pltpu.roll(trace, 0, 1, stride=1, stride_axis=0)
            parts.append(jnp.where(keep, rolled, 0.0).astype(jnp.bfloat16))
        blocks.append(jnp.concatenate(parts, axis=1))
    toeplitz = jnp.concatenate(blocks, axis=0)
    contract = (((1,), (1,)), ((), ()))
    near = lax.dot_general(toeplitz, partners, contract, preferred_element_type=jnp.float32)
    far = lax.dot_general(toeplitz, beyond, contract, preferred_element_type=jnp.float32)
    for r in range(SUB):
        first = r * lag_dev
        skip = r + 1
        columns = [
            near[first : first + lag_dev, k * LANES : (k + 1) * LANES] for k in range(OFF // LANES)
        ]
        columns[0] = jnp.where(lane < skip, far[first : first + lag_dev], columns[0])
        columns = [(c * norm_scale).astype(jnp.bfloat16).astype(jnp.float32) for c in columns]
        turned = [pltpu.roll(column, LANES - skip, 1) for column in columns]
        for k in range(len(columns)):
            following = turned[(k + 1) % len(columns)]
            value = jnp.where(lane < LANES - skip, turned[k], following)
            out_ref[r, :, k * LANES : (k + 1) * LANES] = value.astype(jnp.bfloat16)


def correlate(extended, channels, windows, lag_dev):
    depth = extended.shape[1]
    samples = depth // windows
    return pl.pallas_call(
        functools.partial(correlate_kernel, windows, samples, lag_dev),
        out_shape=jax.ShapeDtypeStruct((channels, lag_dev, OFF), jnp.bfloat16),
        grid=(channels // SUB,),
        in_specs=[pl.BlockSpec(extended.shape, lambda g: (0, 0))],
        out_specs=pl.BlockSpec((SUB, lag_dev, OFF), lambda g: (g, 0, 0)),
        scratch_shapes=[pltpu.VMEM((channels - SUB + OFF + LANES, depth), jnp.bfloat16)],
        compiler_params=pltpu.CompilerParams(vmem_limit_bytes=VMEM_GRANT),
        name="correlate",
    )(extended)


def sweep_kernel(windows, samples, traces, plane, out_ref, staged, ship_sem):
    channels, lag_dev, _ = staged.shape
    lane = lax.broadcasted_iota(jnp.int32, (SUB, LANES), 1)
    half = SUB // 2
    groups = channels // (2 * SUB)
    steps = lag_dev // (2 * SUB) * groups

    def place(turn):
        step, odd = divmod(turn, 2)
        return (2 * (step % groups) + odd) * SUB, 2 * (step // groups)

    def held(turn):
        channel, low = place(turn)
        return channel // LANES, low

    def weights(turn, band, first_lane, count):
        channel, low = place(turn)
        start = (low + band) * SUB
        lanes = channel // LANES * LANES + first_lane
        return jnp.concatenate(
            [plane[w, start : start + samples, lanes : lanes + count] for w in range(windows)], axis=0
        )

    def finish(turn, accs, i):
        channel, low = place(turn)
        part, k = divmod(i, half)
        near = [pltpu.matmul_pop(accs[turn % 2][unit][part][k]) for unit in range(2)]
        far = pltpu.matmul_pop(accs[turn % 2][part][2][k])
        skip = (channel + i) % LANES + 1
        for band in range(2):
            columns = [
                near[band][:, :LANES],
                near[band][:, LANES:],
                far[:, band * LANES : (band + 1) * LANES],
            ]
            values = [
                pltpu.roll(
                    jnp.where(lane < skip, columns[k + 1], columns[k]).astype(jnp.bfloat16),
                    LANES - skip,
                    1,
                )
                for k in range(2)
            ]
            first = (low + band) * SUB
            staged[channel + i, first : first + SUB, :] = jnp.concatenate(values, axis=1)

    def launch(turn, accs):
        channel, _ = place(turn)
        odd = turn % 2
        kept = turn and held(turn) == held(turn - 1)
        if not odd and not kept:
            for unit in range(2):
                pltpu.matmul_push_rhs(weights(turn, unit, 0, OFF), 0, unit)
        count = done = 0
        for kind in (2, 0, 1) if odd else (0, 1, 2):
            for i in range(half):
                staged_rhs = None
                if i == 0 and kind == 0 and (odd or not kept):
                    staged_rhs = 0
                elif i == 0 and kind == 2 and not odd:
                    staged_rhs = 1
                for unit in range(2):
                    part = unit if kind == 2 else kind
                    pltpu.matmul_acc_lhs(
                        accs[odd][unit][kind][i],
                        traces[channel + part * half + i],
                        load_staged_rhs=staged_rhs,
                    )
                if i == 0 and kind == 0 and not odd:
                    for unit in range(2):
                        far = [weights(turn, band, OFF, LANES) for band in range(2)]
                        pltpu.matmul_push_rhs(jnp.concatenate(far, axis=1), 1, unit)
                if i == 0 and kind == 2 and odd:
                    for unit in range(2):
                        pltpu.matmul_push_rhs(weights(turn, unit, 0, OFF), 0, unit)
                count += 1
                while turn and done < SUB * count // (3 * half):
                    finish(turn - 1, accs, done)
                    done += 1

    def ship(turn, first=0, count=SUB):
        channel, low = place(turn)
        where = (pl.ds(channel + first, count), pl.ds(low * SUB, 2 * SUB), slice(None))
        slot = turn + (first > 0)
        return pltpu.make_async_copy(staged.at[where], out_ref.at[where], ship_sem.at[slot])

    def run(*flat):
        flat = iter(flat)
        accs = [[[None] * 3 for _ in range(2)] for _ in range(2)]
        for odd in range(2):
            for unit in range(2):
                for kind in range(3):
                    accs[odd][unit][kind] = [next(flat) for _ in range(half)]
        for turn in range(2 * steps):
            launch(turn, accs)
            if turn:
                ship(turn - 1).start()
        for i in range(SUB):
            finish(2 * steps - 1, accs, i)
            if i == half - 1:
                ship(2 * steps - 1, 0, half).start()
        ship(2 * steps - 1, half, half).start()

    pl.run_scoped(
        run,
        *[
            pltpu.ACC(unit)((SUB, OFF), jnp.float32)
            for odd in range(2)
            for unit in range(2)
            for _ in range(3 * half)
        ],
    )
    for turn in range(2 * steps - 1):
        ship(turn).wait()
    ship(2 * steps - 1, 0, half).wait()
    ship(2 * steps - 1, half, half).wait()


def sweep(traces, plane, lag_dev):
    channels, _, depth = traces.shape
    windows = plane.shape[0]
    turns = lag_dev // (2 * SUB) * (channels // SUB)
    vmem = pl.BlockSpec(memory_space=pltpu.VMEM)
    return pl.pallas_call(
        functools.partial(sweep_kernel, windows, depth // windows),
        out_shape=jax.ShapeDtypeStruct((channels, lag_dev, OFF), jnp.bfloat16),
        in_specs=[vmem, vmem],
        out_specs=pl.BlockSpec(memory_space=pltpu.HBM),
        scratch_shapes=[
            pltpu.VMEM((channels, lag_dev, OFF), jnp.bfloat16),
            pltpu.SemaphoreType.DMA((turns + 1,)),
        ],
        compiler_params=pltpu.CompilerParams(vmem_limit_bytes=VMEM_GRANT),
        name="sweep",
    )(traces, plane)


def shards(raw_strain, fir_taps, live_mask):
    n_chan = lax.axis_size("chan")
    n_tm = lax.axis_size("tm")
    channels = live_mask.shape[0]
    lag_dev = 2 * LAG // n_tm
    samples = raw_strain.shape[2] * n_chan // STRIDE
    swept = n_tm == 2 and samples == LAG == LANES and 2 * samples == OFF
    swept = swept and channels % (2 * SUB) == 0 and channels <= STAGED_CHANNELS
    prepared = prepare(raw_strain, fir_taps, live_mask, n_chan, n_tm, swept)
    if swept:
        return sweep(*prepared, lag_dev)
    return correlate(*prepared, channels, n_tm, lag_dev)


def solution(mesh):
    placed = (P("tm", "fibre", "chan"), P(), P(("fibre", "chan")))
    return jax.shard_map(
        shards,
        mesh=mesh,
        in_specs=placed,
        out_specs=P(("fibre", "chan"), "tm", None),
        check_vma=False,
    )
```
